512 devices in a mesh: dp: 64 (over x, z), tensor: 8 (over y, core).
Axes of the slice: x: 4, y: 4, z: 16, core: 2. Of those that a mesh axis runs over, the one named last changes fastest.
Arguments:
- tokens: bfloat16 [8192, 8192], P('dp', 'tensor'), may hold values from -6 to 6
- hidden_grad: bfloat16 [8192, 28672], P('dp', 'tensor'), may hold values from -0.0625 to 0.0625
- masters: float32 [8, 64, 128, 128], P('tensor', 'dp'), may hold values from -0.5 to 0.5
- block_row: int32 [8, 32], P('tensor'), may hold values from 0 to 63, as said below
- block_col: int32 [8, 32], P('tensor'), may hold values from 0 to 27
- owners: int32 [8, 64], P('tensor'), may hold values from 0 to 63, as said below
Outputs:
- grads: float32 [8, 192, 128, 128], P('tensor', 'dp')
The draws below stay inside these ranges and needn't reach their ends.
Inputs may be any that keep to these rules, and one draw needn't show every extreme that they name: `block_row`: in each slice the kept places are distinct. `owners`: in each slice every owner takes at most 3 of the 64 kept blocks, and some owner takes exactly 3.
All inputs are finite; a program needn't handle non-finite values.
Results may differ from the reference program's by a relative error of at most 0.0044.
Values may be sent and summed in bfloat16 or wider, within the bound.
A program may use at most 64 MiB of HBM per device.

```python
import jax
import jax.numpy as jnp
from jax import lax

D = 8192
FF = 28672
B = 128
KP = 32
TOKENS = 8192
SLICES = 8
OWNERS = 64
KB2 = 64
CAP = 3
NRB = 64
NCB = 28


def place_blocks(key):

    def one_slice(slice_key):
        key_a, key_b, key_c, key_d = jax.random.split(slice_key, 4)
        column_order = jax.random.permutation(key_a, NCB).astype(jnp.int32)
        position = jnp.arange(KP, dtype=jnp.int32)
        column_index = jnp.take(column_order, position % NCB).astype(jnp.int32)
        first_rows = jax.random.randint(key_b, (KP,), 0, NRB, dtype=jnp.int32)
        marked = jax.random.randint(key_c, (), 0, min(KP, NCB), dtype=jnp.int32)
        first_rows = jnp.where(position == marked, NRB - 1, first_rows).astype(jnp.int32)
        offsets = jax.random.randint(key_d, (KP,), 1, NRB, dtype=jnp.int32)
        partner = jnp.take(first_rows, jnp.maximum(position - NCB, 0))
        row_index = jnp.where(position < NCB, first_rows, (partner + offsets) % NRB).astype(jnp.int32)
        return (row_index, column_index)
    return jax.vmap(one_slice)(jax.random.split(key, SLICES))


def draw_block_row(key, part):
    return place_blocks(jax.random.fold_in(key, 11))[0]


def draw_block_col(key, part):
    return place_blocks(jax.random.fold_in(key, 11))[1]


def draw_owners(key, part):

    def one_slice(slice_key):
        key_a, key_b, key_c = jax.random.split(slice_key, 3)
        full_owner = jax.random.randint(key_a, (), 0, OWNERS, dtype=jnp.int32)
        others = jax.random.permutation(key_b, (OWNERS - 1) * CAP)[:KB2 - CAP].astype(jnp.int32)
        others = jnp.where(others >= full_owner * CAP, others + CAP, others).astype(jnp.int32)
        slot_list = jnp.concatenate([full_owner * CAP + jnp.arange(CAP, dtype=jnp.int32), others])
        shuffled = jax.random.permutation(key_c, slot_list)
        return (shuffled // CAP).astype(jnp.int32)
    return jax.vmap(one_slice)(jax.random.split(jax.random.fold_in(key, 23), SLICES))


def steps_of(stream_key, shape, pieces, least, top_value):
    level, own = 1.0, jax.random.fold_in(stream_key, 6)
    for dim, shards_of in pieces:
        heights = jnp.exp(jax.random.uniform(jax.random.fold_in(own, dim), (shards_of,), jnp.float32, least / len(pieces), top_value / len(pieces)))
        level = level * jnp.repeat(heights, shape[dim] // shards_of).reshape([-1 if axis == dim else 1 for axis in range(len(shape))])
    return level


def bell_draw(rng, dims, deviation, limit, cuts=(), kind=jnp.bfloat16):
    level = steps_of(rng, dims, cuts, -0.22, 0.18) if cuts else 1.0
    values = jax.random.normal(rng, dims, jnp.float32) * deviation * level
    return jnp.minimum(jnp.maximum(values, -limit), limit).astype(kind)


def setup_inputs(seed: int = 0) -> dict:
    key_list = jax.random.split(jax.random.key(seed), 7)
    tokens = bell_draw(key_list[0], (TOKENS, D), 1.0, 6.0, ((0, 64), (1, 8)))
    hidden_grad = bell_draw(key_list[1], (TOKENS, FF), TOKENS ** -0.5, 0.0625, ((0, 64), (1, 8)))
    masters = bell_draw(key_list[2], (SLICES, KB2, B, B), B ** -0.5, 0.5, ((0, 8), (1, 64)), jnp.float32)
    block_row = draw_block_row(jax.random.fold_in(key_list[6], 71), 0)
    block_col = draw_block_col(jax.random.fold_in(key_list[6], 71), 0)
    owners = draw_owners(jax.random.fold_in(key_list[6], 71), 0)
    return dict(tokens=tokens, hidden_grad=hidden_grad, masters=masters, block_row=block_row, block_col=block_col, owners=owners)


def slot_index(owner_row, capacity):
    count_all = owner_row.shape[0]
    same_owner = owner_row[:, None] == owner_row[None, :]
    earlier = jnp.arange(count_all, dtype=jnp.int32)[None, :] < jnp.arange(count_all, dtype=jnp.int32)[:, None]
    rank_index = jnp.sum(jnp.logical_and(same_owner, earlier).astype(jnp.int32), axis=1, dtype=jnp.int32)
    return owner_row * capacity + rank_index


def one_slice(tokens, grad_slice, weights, row_index, column_index):
    token_count = tokens.shape[0]
    high = lax.Precision.HIGHEST
    by_block = tokens.reshape(token_count, NRB, B)
    selected = jnp.take(by_block, row_index, axis=1).astype(jnp.float32)
    gate_part = jnp.einsum("tkb,kbc->ktc", selected, weights[:KP].astype(jnp.float32), precision=high)
    up_part = jnp.einsum("tkb,kbc->ktc", selected, weights[KP:].astype(jnp.float32), precision=high)
    gate_cols = jax.ops.segment_sum(gate_part, column_index, num_segments=NCB)
    up_cols = jax.ops.segment_sum(up_part, column_index, num_segments=NCB)
    grad_cols = jnp.moveaxis(grad_slice.reshape(token_count, NCB, B), 1, 0).astype(jnp.float32)
    sigmoid_gate = jax.nn.sigmoid(gate_cols)
    gate_grad = (grad_cols * up_cols * sigmoid_gate * (1.0 + gate_cols * (1.0 - sigmoid_gate))).astype(jnp.bfloat16)
    up_grad = (grad_cols * gate_cols * sigmoid_gate).astype(jnp.bfloat16)
    gate_blocks = jnp.take(gate_grad, column_index, axis=0).astype(jnp.float32)
    up_blocks = jnp.take(up_grad, column_index, axis=0).astype(jnp.float32)
    grad_gate = jnp.einsum("tkb,ktc->kbc", selected, gate_blocks, precision=high)
    grad_up = jnp.einsum("tkb,ktc->kbc", selected, up_blocks, precision=high)
    return jnp.concatenate([grad_gate, grad_up], axis=0)


def reference(tokens, hidden_grad, masters, block_row, block_col, owners):
    weights = masters.astype(jnp.bfloat16)
    slice_width = FF // SLICES

    def per_slice(slice_number):
        grad_slice = lax.dynamic_slice_in_dim(hidden_grad, slice_number * slice_width, slice_width, 1)
        return one_slice(tokens, grad_slice, weights[slice_number], block_row[slice_number], block_col[slice_number])

    block_grads = lax.map(per_slice, jnp.arange(SLICES, dtype=jnp.int32))
    slot_list = jax.vmap(lambda owner_row: slot_index(owner_row, CAP))(owners)
    result = jnp.zeros((SLICES, OWNERS * CAP, B, B), jnp.float32)
    slice_numbers = jnp.arange(SLICES, dtype=jnp.int32)[:, None]
    return result.at[slice_numbers, slot_list].set(block_grads)
```

```python
import functools

import jax
import jax.numpy as jnp
from jax import lax
from jax.experimental import pallas as pl
from jax.experimental.pallas import tpu as pltpu
from jax.sharding import PartitionSpec as P

MESH = pl.DeviceIdType.MESH
X, Z, Y, CORES = 4, 16, 4, 2
B = 128
KP = 32
CAP = 3
F32, BF16 = jnp.float32, jnp.bfloat16
VMEM = pl.BlockSpec(memory_space=pltpu.VMEM)
SMEM = pl.BlockSpec(memory_space=pltpu.SMEM)
DMA = pltpu.SemaphoreType.DMA
STEPS = (2, 1, -1, 0)


def place():
    dp, t = lax.axis_index("dp"), lax.axis_index("tensor")
    return dp // Z, lax.rem(dp, Z), t


def x_peer(x, z, t, step):
    return (lax.rem(x + step + X, X) * Z + z, t)


def z_peer(x, z, t, step):
    return (x * Z + lax.rem(z + step + Z, Z), t)


def y_peer(x, z, t, step):
    return (x * Z + z, lax.rem(t + CORES * step + Y * CORES, Y * CORES))


def core_peer(x, z, t):
    return (x * Z + z, t + 1 - 2 * lax.rem(t, CORES))


def meet(peers):
    barrier = pltpu.get_barrier_semaphore()
    for peer in peers:
        pl.semaphore_signal(barrier, inc=1, device_id=peer, device_id_type=MESH)
    pl.semaphore_wait(barrier, len(peers))


def send(src, dst, send_sem, recv_sem, peer):
    return pltpu.make_async_remote_copy(
        src_ref=src, dst_ref=dst, send_sem=send_sem, recv_sem=recv_sem,
        device_id=peer, device_id_type=MESH,
    )


def gather_kernel(tokens, masters, feats, weights, own, xs, xr, zs, zr, ys, yr, cs, cr):
    x, z, t = place()
    meet(
        [x_peer(x, z, t, s) for s in (1, 2, 3)]
        + [z_peer(x, z, t, s) for s in (1, -1)]
        + [y_peer(x, z, t, s) for s in (1, 2, 3)]
        + [core_peer(x, z, t)]
    )
    own[...] = masters[...].astype(BF16)
    spot = (z * 2 + lax.rem(x, 2), slice(None), pl.ds(pl.multiple_of(x // 2 * B, B), B))
    moves = []
    first = [
        send(own, weights.at[spot], xs.at[s - 1], xr.at[s - 1], x_peer(x, z, t, s))
        for s in (1, 3, 2)
    ]
    for copy in first:
        copy.start()
    y_moves = {
        s: send(tokens, feats.at[t], ys.at[s - 1], yr.at[s - 1], y_peer(x, z, t, s))
        for s in (1, 3, 2)
    }
    for copy in y_moves.values():
        copy.start()
    over = send(tokens, feats.at[t], cs.at[0], cr.at[0], core_peer(x, z, t))
    over.start()
    weights[spot] = own[...]
    feats[t] = tokens[...]
    for copy in first:
        copy.wait_recv()

    def hop(way, step, part):
        sign = 1 - 2 * way
        index = lax.rem(z - sign * step + 2 * Z, Z) * 2 + part
        return send(
            weights.at[index], weights.at[index],
            zs.at[way, step, part], zr.at[way, step, part], z_peer(x, z, t, sign),
        )

    def hops(step):
        if step < 7:
            return [(way, part) for part in (0, 1) for way in (0, 1)]
        return [(0, 0), (1, 1)]

    sent = []
    waiting = []
    for step in range(8):
        now = []
        for way, part in hops(step):
            if step:
                hop(way, step - 1, part).wait_recv()
            copy = hop(way, step, part)
            copy.start()
            now.append(copy)
        if step == 7:
            for way, part in ((0, 1), (1, 0)):
                hop(way, 6, part).wait_recv()
        sent += now
        if step in (3, 4, 5):
            s = {3: 1, 4: 3, 5: 2}[step]
            y_moves[s].wait_recv()
            source = lax.rem(t - CORES * s + Y * CORES, Y * CORES)
            copy = send(feats.at[source], feats.at[source], cs.at[s], cr.at[s], core_peer(x, z, t))
            copy.start()
            waiting.append(copy)
    for copy in now:
        copy.wait_recv()
    over.wait_recv()
    for copy in waiting:
        copy.wait_recv()
    for copy in sent + first + list(y_moves.values()) + [over] + waiting:
        copy.wait_send()


def compute_kernel(meta, keep, feats, weights, hidden, out, part, grads):
    def selected(i):
        return feats[meta[0, i], :, pl.ds(pl.multiple_of(meta[1, i], B), B)]

    def forward(i):
        value = jnp.dot(selected(i), weights[meta[2, i]], preferred_element_type=F32)
        part[i + 1] = part[i] * keep[i] + value

    part[0] = jnp.zeros_like(part[0])

    @pl.loop(0, KP, unroll=4)
    def _(i):
        forward(i)

    def backward(i):
        last = meta[3, i]
        gate = part[last, :, :B]
        up = part[last, :, B:]
        upstream = hidden[:, pl.ds(pl.multiple_of(meta[4, i], B), B)].astype(F32)
        sig = 1.0 / (1.0 + jnp.exp(-gate))
        gate_grad = upstream * up * sig * (1.0 + gate * (1.0 - sig))
        up_grad = upstream * gate * sig
        grads[:, :B] = gate_grad.astype(BF16)
        grads[:, B:] = up_grad.astype(BF16)
        total = lax.dot_general(
            selected(i), grads[...], (((0,), (0,)), ((), ())), preferred_element_type=F32
        )
        at = pl.ds(pl.multiple_of(i * 16, 16), 16)
        for p in range(16):
            rows = total[8 * p : 8 * p + 8]
            out[p, at] = jnp.concatenate([rows[:, :B], rows[:, B:]], axis=0).astype(BF16)

    @pl.loop(0, KP, unroll=2)
    def _(i):
        backward(i)


def reduce_kernel(
    inverse, partial, out, got, near_out, near_in, mine, owner_out, owner_in, final_out,
    xs, xr, ns, nr, os, ors, fs, fr,
):
    x, z, t = place()
    meet(
        [x_peer(x, z, t, s) for s in (1, 2, 3)]
        + [z_peer(x, z, t, s) for s in range(1, Z)]
    )
    half = KP * 8

    def x_copy(j, s):
        piece = lax.rem(x + s, X) * 4 + lax.rem(z + STEPS[j] + Z, 4)
        return send(
            partial.at[piece], got.at[j, s - 1], xs.at[j, s - 1], xr.at[j, s - 1],
            x_peer(x, z, t, s),
        )

    x_copies = [[x_copy(j, s) for s in (1, 3, 2)] for j in range(4)]
    for row in x_copies:
        for copy in row:
            copy.start()

    def near_copies(j):
        if j == 0:
            return [
                send(near_out.at[0, pl.ds(0, half)], near_in.at[0, pl.ds(0, half)],
                     ns.at[0], nr.at[0], z_peer(x, z, t, 2)),
                send(near_out.at[0, pl.ds(half, half)], near_in.at[0, pl.ds(half, half)],
                     ns.at[3], nr.at[3], z_peer(x, z, t, -2)),
            ]
        return [send(near_out.at[j], near_in.at[j], ns.at[j], nr.at[j], z_peer(x, z, t, STEPS[j]))]

    near = []
    tile = 64
    for j in range(4):
        for copy in x_copies[j]:
            copy.wait_recv()
        piece = x * 4 + lax.rem(z + STEPS[j] + Z, 4)

        @pl.loop(0, 2 * half // tile)
        def _(r):
            at = pl.ds(pl.multiple_of(r * tile, tile), tile)
            total = partial[piece, at].astype(F32)
            for s in range(3):
                total += got[j, s, at].astype(F32)
            if j < 3:
                near_out[j, at] = total.astype(BF16)
            else:
                mine[pl.ds(r * 8, 8)] = total.reshape(8, 8, B)

        if j < 3:
            for copy in near_copies(j):
                copy.start()
                near.append(copy)
    for copy in near:
        copy.wait_recv()

    @pl.loop(0, 2 * half // tile)
    def _(r):
        at = pl.ds(pl.multiple_of(r * tile, tile), tile)
        blocks = pl.ds(r * 8, 8)
        total = mine[blocks].reshape(tile, B)
        for j in range(3):
            total += near_in[j, at].astype(F32)
        mine[blocks] = total.reshape(8, 8, B)

    mine[2 * KP] = jnp.zeros((8, B), F32)

    def slot(zo, q):
        number = (q // CAP * Z + zo) * CAP + q % CAP
        return mine[inverse[number]]

    owner_copies = []
    for step in [8, 7, 9, 6, 10, 5, 11, 4, 12, 3, 13, 2, 14, 1, 15, 0]:
        zo = lax.rem(z + step, Z)
        for q in range(0, 12, 2):
            owner_out[step, 8 * q : 8 * q + 16] = jnp.concatenate(
                [slot(zo, q), slot(zo, q + 1)], axis=0
            ).astype(BF16)
        if step:
            copy = send(owner_out.at[step], owner_in.at[step], os.at[step], ors.at[step],
                        z_peer(x, z, t, step))
            copy.start()
            owner_copies.append(copy)
    for copy in owner_copies:
        copy.wait_recv()
    for e in range(4):
        total = owner_out[0] if e == 0 else owner_in[e]
        total = total.astype(F32)
        for k in (4, 8, 12):
            total += owner_in[e + k].astype(F32)
        row = pl.multiple_of(lax.rem(z - e + Z, 4) * 8, 8)
        for q in range(12):
            final_out[q // CAP, q % CAP, pl.ds(row, 8)] = total[8 * q : 8 * q + 8]
    rows = pl.ds(pl.multiple_of(x * 32, 32), 32)
    final = [
        send(final_out.at[lax.rem(x + s, X)], out.at[:, rows], fs.at[s - 1], fr.at[s - 1],
             x_peer(x, z, t, s))
        for s in (1, 3, 2)
    ]
    for copy in final:
        copy.start()
    out[:, rows] = final_out[x]
    for copy in final:
        copy.wait_recv()
    for copy in sum(x_copies, []) + near + owner_copies + final:
        copy.wait_send()


def tables(rows, columns, owners):
    places = jnp.arange(KP, dtype=jnp.int32)
    before = (columns[None, :] < columns[:, None]) | (
        (columns[None, :] == columns[:, None]) & (places[None, :] < places[:, None])
    )
    rank = jnp.sum(before.astype(jnp.int32), axis=1)
    hit = (rank[None, :] == places[:, None]).astype(jnp.int32)
    order = jnp.sum(hit * places[None, :], axis=1)
    row = jnp.sum(hit * rows[None, :], axis=1)
    column = jnp.sum(hit * columns[None, :], axis=1)
    upto = jnp.sum((columns[None, :] <= column[:, None]).astype(jnp.int32), axis=1)
    first = jnp.sum((columns[None, :] < column[:, None]).astype(jnp.int32), axis=1)
    keep = (first != places).astype(F32)
    meta = jnp.stack(
        [row // 8, row % 8 * B, order % Z * 2 + order // Z, upto, column * B]
    )
    blocks = jnp.arange(2 * KP, dtype=jnp.int32)
    earlier = (owners[None, :] == owners[:, None]) & (blocks[None, :] < blocks[:, None])
    slots = owners * CAP + jnp.sum(earlier.astype(jnp.int32), axis=1)
    position = jnp.concatenate([rank * 2, rank * 2 + 1])
    taken = slots[None, :] == jnp.arange(X * Z * CAP, dtype=jnp.int32)[:, None]
    inverse = jnp.sum(jnp.where(taken, position[None, :] - 2 * KP, 0), axis=1) + 2 * KP
    return meta, keep, inverse


def local(tokens, hidden_grad, masters, block_row, block_col, owners):
    meta, keep, inverse = tables(block_row[0], block_col[0], owners[0])
    limit = 56 << 20
    feats, weights = pl.pallas_call(
        gather_kernel,
        name="gather",
        out_shape=[
            jax.ShapeDtypeStruct((Y * CORES, B, 8 * B), BF16),
            jax.ShapeDtypeStruct((KP, B, 2 * B), BF16),
        ],
        in_specs=[VMEM, VMEM],
        out_specs=[VMEM, VMEM],
        scratch_shapes=[pltpu.VMEM((B, B), BF16), DMA((3,)), DMA((3,)), DMA((2, 8, 2)), DMA((2, 8, 2)),
                        DMA((3,)), DMA((3,)), DMA((4,)), DMA((4,))],
        compiler_params=pltpu.CompilerParams(
            collective_id=0, has_side_effects=True, vmem_limit_bytes=limit
        ),
    )(tokens, masters.reshape(B, B))
    partial = pl.pallas_call(
        compute_kernel,
        name="compute",
        out_shape=jax.ShapeDtypeStruct((16, KP * 16, B), BF16),
        in_specs=[SMEM, SMEM, VMEM, VMEM, VMEM],
        out_specs=VMEM,
        scratch_shapes=[pltpu.VMEM((KP + 1, B, 2 * B), F32), pltpu.VMEM((B, 2 * B), BF16)],
        compiler_params=pltpu.CompilerParams(vmem_limit_bytes=limit),
    )(meta, keep, feats, weights, hidden_grad)
    size = KP * 16
    result = pl.pallas_call(
        reduce_kernel,
        name="reduce",
        out_shape=jax.ShapeDtypeStruct((CAP, B, B), F32),
        in_specs=[SMEM, VMEM],
        out_specs=VMEM,
        scratch_shapes=[
            pltpu.VMEM((4, 3, size, B), BF16),
            pltpu.VMEM((3, size, B), BF16),
            pltpu.VMEM((3, size, B), BF16),
            pltpu.VMEM((2 * KP + 1, 8, B), F32),
            pltpu.VMEM((Z, 96, B), BF16),
            pltpu.VMEM((Z, 96, B), BF16),
            pltpu.VMEM((X, CAP, 32, B), F32),
            DMA((4, 3)), DMA((4, 3)), DMA((4,)), DMA((4,)), DMA((Z,)), DMA((Z,)), DMA((3,)), DMA((3,)),
        ],
        compiler_params=pltpu.CompilerParams(
            collective_id=1, has_side_effects=True, vmem_limit_bytes=limit
        ),
    )(inverse, partial)
    return result[None]


def solution(mesh):
    return jax.shard_map(
        local,
        mesh=mesh,
        in_specs=(
            P("dp", "tensor"),
            P("dp", "tensor"),
            P("tensor", "dp", None, None),
            P("tensor", None),
            P("tensor", None),
            P("tensor", None),
        ),
        out_specs=P("tensor", "dp", None, None),
        check_vma=False,
    )
```

```python
import functools

import jax
import jax.numpy as jnp
from jax import lax
from jax.experimental import pallas as pl
from jax.experimental.pallas import tpu as pltpu
from jax.sharding import PartitionSpec as P

MESH = pl.DeviceIdType.MESH
X, Z, Y, CORES = 4, 16, 4, 2
B = 128
KP = 32
CAP = 3
F32, BF16 = jnp.float32, jnp.bfloat16
VMEM = pl.BlockSpec(memory_space=pltpu.VMEM)
SMEM = pl.BlockSpec(memory_space=pltpu.SMEM)
DMA = pltpu.SemaphoreType.DMA
STEPS = (2, 1, -1, 0)
XSTEPS = (2, 1, 3, 0)
HALF = KP // 2


def place():
    dp, t = lax.axis_index("dp"), lax.axis_index("tensor")
    return dp // Z, lax.rem(dp, Z), t


def x_peer(x, z, t, step):
    return (lax.rem(x + step + X, X) * Z + z, t)


def z_peer(x, z, t, step):
    return (x * Z + lax.rem(z + step + Z, Z), t)


def y_peer(x, z, t, step):
    return (x * Z + z, lax.rem(t + CORES * step + Y * CORES, Y * CORES))


def core_peer(x, z, t):
    return (x * Z + z, t + 1 - 2 * lax.rem(t, CORES))


def greet(peers):
    barrier = pltpu.get_barrier_semaphore()
    for peer in peers:
        pl.semaphore_signal(barrier, inc=1, device_id=peer, device_id_type=MESH)
    return lambda: pl.semaphore_wait(barrier, len(peers))


def send(src, dst, send_sem, recv_sem, peer):
    return pltpu.make_async_remote_copy(
        src_ref=src, dst_ref=dst, send_sem=send_sem, recv_sem=recv_sem,
        device_id=peer, device_id_type=MESH,
    )


def total(mask, values, axis):
    return jnp.sum(jnp.where(mask, values, 0), axis=axis, keepdims=True)


def tables(rows, columns, owners):
    i32 = jnp.int32

    def grid(a, b, dim):
        return lax.broadcasted_iota(i32, (a, b), dim)

    sub, lane = grid(KP, KP, 0), grid(KP, KP, 1)
    col_t, row_t = total(sub == lane, columns, 1), total(sub == lane, rows, 1)
    before = (columns < col_t) | ((columns == col_t) & (lane < sub))
    rank_t = jnp.sum(before.astype(i32), axis=1, keepdims=True)
    sub, lane = grid(KP, B, 0), grid(KP, B, 1)
    hit = rank_t == lane
    order = total(hit, sub, 0)
    row_s = total(hit, row_t, 0)
    col_s = total(hit, col_t, 0)
    upto = jnp.sum((col_t <= col_s).astype(i32), axis=0, keepdims=True)
    first = jnp.sum((col_t < col_s).astype(i32), axis=0, keepdims=True)
    keep = (first != lax.broadcasted_iota(i32, (1, B), 1)).astype(i32)
    n = 2 * KP
    sub, lane = grid(n, n, 0), grid(n, n, 1)
    own_t = total(sub == lane, owners, 1)
    earlier = (owners == own_t) & (lane < sub)
    slot_t = own_t * CAP + jnp.sum(earlier.astype(i32), axis=1, keepdims=True)
    sub, lane = grid(n, KP, 0), grid(n, KP, 1)
    which = lax.rem(sub, KP)
    col_n = total(which == lane, columns, 1)
    before = (columns < col_n) | ((columns == col_n) & (lane < which))
    position = 2 * jnp.sum(before.astype(i32), axis=1, keepdims=True)
    position += (grid(n, 1, 0) >= KP).astype(i32)
    taken = slot_t == grid(n, 2 * B, 1)
    inverse = n + total(taken, position - n, 0)
    return order, row_s, col_s, upto, keep, inverse


def fused(
    tokens, hidden, masters, rows, columns, owners, out,
    own, feats, weights, hidden_raw, hid, table, meta, raw, part, grads,
    part_a, part_b, in_a, in_b, out_a, out_b, in_a2, in_b2, mine, owner_out, owner_in, final_out,
    local_sem, xs, xr, zs, zr, ys, yr, cs, cr,
    as_, ar, bs, br, as2, ar2, bs2, br2, os, ors, fs, fr,
):
    x, z, t = place()
    wait_all = greet(
        [x_peer(x, z, t, s) for s in (1, 2, 3)]
        + [z_peer(x, z, t, s) for s in range(1, Z)]
        + [y_peer(x, z, t, s) for s in (1, 2, 3)]
        + [core_peer(x, z, t)]
    )
    bring = pltpu.make_async_copy(hidden, hidden_raw, local_sem.at[0])
    bring.start()
    own[...] = masters[...].astype(BF16)
    spot = (z * 2 + lax.rem(x, 2), slice(None), pl.ds(pl.multiple_of(x // 2 * B, B), B))
    weights[spot] = own[...]
    for j in range(8):
        feats[t * 8 + j] = tokens[:, j * B : j * B + B]
    my_feats = feats.at[pl.ds(t * 8, 8)]
    wait_all()

    first = [
        send(own, weights.at[spot], xs.at[s - 1], xr.at[s - 1], x_peer(x, z, t, s))
        for s in (1, 3, 2)
    ]
    for copy in first:
        copy.start()
    y_moves = {
        s: send(my_feats, my_feats, ys.at[s - 1], yr.at[s - 1], y_peer(x, z, t, s))
        for s in (1, 3, 2)
    }
    for copy in y_moves.values():
        copy.start()
    over = send(my_feats, my_feats, cs.at[0], cr.at[0], core_peer(x, z, t))
    over.start()

    order, row_s, col_s, upto, keep, inverse = tables(rows[...], columns[...], owners[...])
    for r, value in enumerate((order, row_s, col_s, upto, keep)):
        table[r : r + 1, :B] = value
    table[5:6, :] = inverse
    table[6:7, :KP] = rows[...]
    to_scalar = pltpu.make_async_copy(table, meta, local_sem.at[1])
    to_scalar.start()

    for copy in first:
        copy.wait_recv()

    def hop(way, step, half):
        sign = 1 - 2 * way
        index = lax.rem(z - sign * step + 2 * Z, Z) * 2 + half
        return send(
            weights.at[index], weights.at[index],
            zs.at[way, step, half], zr.at[way, step, half], z_peer(x, z, t, sign),
        )

    def hops(step):
        if step < 7:
            return [(way, half) for half in (0, 1) for way in (0, 1)]
        return [(0, 0), (1, 1)]

    def forward(step, half):
        zz = lax.rem(z + step + 2 * Z, Z)
        spot_k = half * Z + zz
        raw[spot_k] = jnp.dot(
            feats[meta[6, spot_k]], weights[zz * 2 + half], preferred_element_type=F32
        )

    sent = []
    passed = []
    for step in range(8):
        now = []
        for way, half in hops(step):
            if step:
                hop(way, step - 1, half).wait_recv()
            copy = hop(way, step, half)
            copy.start()
            now.append(copy)
        if step == 7:
            for way, half in ((0, 1), (1, 0)):
                hop(way, 6, half).wait_recv()
        sent += now
        if step == 0:
            bring.wait()
            for c in range(hid.shape[0]):
                hid[c] = hidden_raw[:, c * B : c * B + B]
        if step == 1:
            to_scalar.wait()
        if step in (3, 4, 5):
            s = {3: 1, 4: 3, 5: 2}[step]
            y_moves[s].wait_recv()
            source = feats.at[pl.ds(lax.rem(t - CORES * s + Y * CORES, Y * CORES) * 8, 8)]
            copy = send(source, source, cs.at[s], cr.at[s], core_peer(x, z, t))
            copy.start()
            passed.append(copy)
        if step == 6:
            over.wait_recv()
            for copy in passed:
                copy.wait_recv()
        if step >= 6:
            early = [0, 1, -1, 2, -2, 3, -3] if step == 6 else [4, -4, 5, -5, 6, -6, 7, -7]
            for distance in early:
                for half in range(2):
                    forward(distance, half)
    for copy in now:
        copy.wait_recv()
    for half in range(2):
        forward(8, half)

    part[0] = jnp.zeros_like(part[0])

    @pl.loop(0, KP)
    def _(i):
        part[i + 1] = part[i] * meta[4, i].astype(F32) + raw[meta[0, i]]

    def backward(i, store):
        last = meta[3, i]
        value = part[last]
        gate, up = value[:, :B], value[:, B:]
        upstream = hid[meta[2, i]].astype(F32)
        sig = 1.0 / (1.0 + jnp.exp(-gate))
        scaled = upstream * sig
        grads[:, :B] = (scaled * up * (1.0 + gate * (1.0 - sig))).astype(BF16)
        grads[:, B:] = (scaled * gate).astype(BF16)
        block = lax.dot_general(
            feats[meta[1, i]], grads[...], (((0,), (0,)), ((), ())), preferred_element_type=F32
        )
        for p in range(16):
            r = block[8 * p : 8 * p + 8]
            store(p, jnp.concatenate([r[:, :B], r[:, B:]], axis=0).astype(BF16))

    @pl.loop(0, HALF)
    def _(i):
        at = pl.ds(pl.multiple_of(i * 16, 16), 16)

        def store(p, v):
            part_a[p, at] = v

        backward(i, store)

    def a_copy(j, s):
        piece = lax.rem(x + s, X) * 4 + lax.rem(z + STEPS[j] + Z, 4)
        return send(
            part_a.at[piece], in_a.at[j, s - 1], as_.at[j, s - 1], ar.at[j, s - 1],
            x_peer(x, z, t, s),
        )

    a_copies = [[a_copy(j, s) for s in (1, 3, 2)] for j in range(4)]
    for group in a_copies:
        for copy in group:
            copy.start()

    @pl.loop(0, HALF)
    def _(i):
        at = pl.ds(pl.multiple_of(i * 16, 16), 16)

        def store(p, v):
            part_b[p, at] = v

        backward(i + HALF, store)

    def b_copy(j, k):
        step = STEPS[k] if k or j % 2 == 0 else -STEPS[k]
        piece = lax.rem(x + XSTEPS[j], X) * 4 + lax.rem(z + step + Z, 4)
        return send(
            part_b.at[piece], in_b.at[j, k], bs.at[j, k], br.at[j, k], z_peer(x, z, t, step)
        )

    b_copies = [[b_copy(j, k) for k in (0, 1, 2)] for j in range(4)]
    for group in b_copies:
        for copy in group:
            copy.start()

    tile = 64
    size = HALF * 16

    def merge(own_piece, arrived, store):
        @pl.loop(0, size // tile)
        def _(r):
            at = pl.ds(pl.multiple_of(r * tile, tile), tile)
            value = own_piece[at].astype(F32)
            for k in range(3):
                value += arrived[k, at].astype(F32)
            store(r, at, value)

    second = []
    for j in range(4):
        def keep_a(r, at, value, j=j):
            if j < 3:
                out_a[j, at] = value.astype(BF16)
            else:
                mine[pl.ds(r * 8, 8)] = value.reshape(8, 8, B)

        def keep_b(r, at, value, j=j):
            if j < 3:
                out_b[j, at] = value.astype(BF16)
            else:
                mine[pl.ds(KP + r * 8, 8)] = value.reshape(8, 8, B)

        for copy in a_copies[j]:
            copy.wait_recv()
        merge(part_a.at[x * 4 + lax.rem(z + STEPS[j] + Z, 4)], in_a.at[j], keep_a)
        if j < 3:
            if j == 0:
                cut = size // 2
                pieces = [(pl.ds(0, cut), 0, 2), (pl.ds(cut, cut), 3, -2)]
            else:
                pieces = [(pl.ds(0, size), j, STEPS[j])]
            for at, sem, step in pieces:
                copy = send(out_a.at[j, at], in_a2.at[j, at], as2.at[sem], ar2.at[sem],
                            z_peer(x, z, t, step))
                copy.start()
                second.append(copy)
        for copy in b_copies[j]:
            copy.wait_recv()
        merge(part_b.at[lax.rem(x + XSTEPS[j], X) * 4 + lax.rem(z, 4)], in_b.at[j], keep_b)
        if j < 3:
            copy = send(out_b.at[j], in_b2.at[j], bs2.at[j], br2.at[j], x_peer(x, z, t, XSTEPS[j]))
            copy.start()
            second.append(copy)
    for copy in second:
        copy.wait_recv()

    for base, arrived in ((0, in_a2), (KP, in_b2)):
        @pl.loop(0, size // tile)
        def _(r):
            at = pl.ds(pl.multiple_of(r * tile, tile), tile)
            blocks = pl.ds(base + r * 8, 8)
            value = mine[blocks].reshape(tile, B)
            for j in range(3):
                value += arrived[j, at].astype(F32)
            mine[blocks] = value.reshape(8, 8, B)

    mine[2 * KP] = jnp.zeros((8, B), F32)

    def slot(zo, q):
        return mine[meta[5, (q // CAP * Z + zo) * CAP + q % CAP]]

    owner_copies = []
    for step in (8, 7, 9, 6, 10, 5, 11, 4, 12, 3, 13, 2, 14, 1, 15, 0):
        zo = lax.rem(z + step, Z)
        for q in range(0, 12, 2):
            owner_out[step, 8 * q : 8 * q + 16] = jnp.concatenate(
                [slot(zo, q), slot(zo, q + 1)], axis=0
            ).astype(BF16)
        if step:
            copy = send(owner_out.at[step], owner_in.at[step], os.at[step], ors.at[step],
                        z_peer(x, z, t, step))
            copy.start()
            owner_copies.append(copy)
    for copy in owner_copies:
        copy.wait_recv()
    for e in range(4):
        value = owner_out[0] if e == 0 else owner_in[e]
        value = value.astype(F32)
        for k in (4, 8, 12):
            value += owner_in[e + k].astype(F32)
        row = pl.multiple_of(lax.rem(z - e + Z, 4) * 8, 8)
        for q in range(12):
            final_out[q // CAP, q % CAP, pl.ds(row, 8)] = value[8 * q : 8 * q + 8]
    block_rows = pl.ds(pl.multiple_of(x * 32, 32), 32)
    final = [
        send(final_out.at[lax.rem(x + s, X)], out.at[:, block_rows], fs.at[s - 1], fr.at[s - 1],
             x_peer(x, z, t, s))
        for s in (1, 3, 2)
    ]
    for copy in final:
        copy.start()
    out[:, block_rows] = final_out[x]
    for copy in final:
        copy.wait_recv()
    done = first + list(y_moves.values()) + [over] + passed + sent
    done += sum(a_copies, []) + sum(b_copies, []) + second + owner_copies + final
    for copy in done:
        copy.wait_send()


def local(tokens, hidden_grad, masters, block_row, block_col, owners):
    size = HALF * 16
    columns = hidden_grad.shape[1] // B
    result = pl.pallas_call(
        fused,
        name="fused",
        out_shape=jax.ShapeDtypeStruct((CAP, B, B), F32),
        in_specs=[VMEM, pl.BlockSpec(memory_space=pl.ANY), VMEM, VMEM, VMEM, VMEM],
        out_specs=VMEM,
        scratch_shapes=[
            pltpu.VMEM((B, B), BF16),
            pltpu.VMEM((Y * CORES * 8, B, B), BF16),
            pltpu.VMEM((KP, B, 2 * B), BF16),
            pltpu.VMEM(hidden_grad.shape, BF16),
            pltpu.VMEM((columns, B, B), BF16),
            pltpu.VMEM((8, 2 * B), jnp.int32),
            pltpu.SMEM((8, 2 * B), jnp.int32),
            pltpu.VMEM((KP, B, 2 * B), F32),
            pltpu.VMEM((KP + 1, B, 2 * B), F32),
            pltpu.VMEM((B, 2 * B), BF16),
            pltpu.VMEM((16, size, B), BF16),
            pltpu.VMEM((16, size, B), BF16),
            pltpu.VMEM((4, 3, size, B), BF16),
            pltpu.VMEM((4, 3, size, B), BF16),
            pltpu.VMEM((3, size, B), BF16),
            pltpu.VMEM((3, size, B), BF16),
            pltpu.VMEM((3, size, B), BF16),
            pltpu.VMEM((3, size, B), BF16),
            pltpu.VMEM((2 * KP + 1, 8, B), F32),
            pltpu.VMEM((Z, 96, B), BF16),
            pltpu.VMEM((Z, 96, B), BF16),
            pltpu.VMEM((X, CAP, 32, B), F32),
            DMA((2,)),
            DMA((3,)), DMA((3,)), DMA((2, 8, 2)), DMA((2, 8, 2)), DMA((3,)), DMA((3,)), DMA((4,)), DMA((4,)),
            DMA((4, 3)), DMA((4, 3)), DMA((4, 3)), DMA((4, 3)), DMA((4,)), DMA((4,)), DMA((3,)), DMA((3,)),
            DMA((Z,)), DMA((Z,)), DMA((3,)), DMA((3,)),
        ],
        compiler_params=pltpu.CompilerParams(
            collective_id=0, has_side_effects=True, vmem_limit_bytes=56 << 20
        ),
    )(tokens, hidden_grad, masters.reshape(B, B), block_row, block_col, owners)
    return result[None]


def solution(mesh):
    return jax.shard_map(
        local,
        mesh=mesh,
        in_specs=(
            P("dp", "tensor"),
            P("dp", "tensor"),
            P("tensor", "dp", None, None),
            P("tensor", None),
            P("tensor", None),
            P("tensor", None),
        ),
        out_specs=P("tensor", "dp", None, None),
        check_vma=False,
    )
```

```python
import functools

import jax
import jax.numpy as jnp
from jax import lax
from jax.experimental import pallas as pl
from jax.experimental.pallas import tpu as pltpu
from jax.sharding import PartitionSpec as P

MESH = pl.DeviceIdType.MESH
X, Z, Y, CORES = 4, 16, 4, 2
B = 128
KP = 32
CAP = 3
F32, BF16 = jnp.float32, jnp.bfloat16
VMEM = pl.BlockSpec(memory_space=pltpu.VMEM)
SMEM = pl.BlockSpec(memory_space=pltpu.SMEM)
DMA = pltpu.SemaphoreType.DMA
STEPS = (2, 1, -1, 0)
XSTEPS = (2, 1, 3, 0)
HALF = KP // 2
LOW = 32
MOVES = (
    (0, 5), (0, -5), (0, 1), (0, -1),
    (-5, 1), (-5, -1), (5, 1), (5, -1), (-1, 1), (1, -1),
    (-6, 1), (4, 1), (-4, -1), (6, -1),
    (-7, 1), (7, -1),
)
STAGES = ((0, 1, 2, 3), (4, 5, 6, 7, 8, 9), (10, 11, 12, 13), (14, 15))


def place():
    dp, t = lax.axis_index("dp"), lax.axis_index("tensor")
    return dp // Z, lax.rem(dp, Z), t


def x_peer(x, z, t, step):
    return (lax.rem(x + step + X, X) * Z + z, t)


def z_peer(x, z, t, step):
    return (x * Z + lax.rem(z + step + Z, Z), t)


def y_peer(x, z, t, step):
    return (x * Z + z, lax.rem(t + CORES * step + Y * CORES, Y * CORES))


def core_peer(x, z, t):
    return (x * Z + z, t + 1 - 2 * lax.rem(t, CORES))


def greet(peers):
    barrier = pltpu.get_barrier_semaphore()
    for peer in peers:
        pl.semaphore_signal(barrier, inc=1, device_id=peer, device_id_type=MESH)
    return lambda: pl.semaphore_wait(barrier, len(peers))


def send(src, dst, send_sem, recv_sem, peer):
    return pltpu.make_async_remote_copy(
        src_ref=src, dst_ref=dst, send_sem=send_sem, recv_sem=recv_sem,
        device_id=peer, device_id_type=MESH,
    )


def total(mask, values, axis):
    return jnp.sum(jnp.where(mask, values, 0), axis=axis, keepdims=True)


def tables(rows, columns, owners):
    i32 = jnp.int32

    def grid(a, b, dim):
        return lax.broadcasted_iota(i32, (a, b), dim)

    sub, lane = grid(KP, KP, 0), grid(KP, KP, 1)
    col_t, row_t = total(sub == lane, columns, 1), total(sub == lane, rows, 1)
    before = (columns < col_t) | ((columns == col_t) & (lane < sub))
    rank_t = jnp.sum(before.astype(i32), axis=1, keepdims=True)
    sub, lane = grid(KP, B, 0), grid(KP, B, 1)
    hit = rank_t == lane
    order = total(hit, sub, 0)
    row_s = total(hit, row_t, 0)
    col_s = total(hit, col_t, 0)
    upto = jnp.sum((col_t <= col_s).astype(i32), axis=0, keepdims=True)
    first = jnp.sum((col_t < col_s).astype(i32), axis=0, keepdims=True)
    keep = (first != lax.broadcasted_iota(i32, (1, B), 1)).astype(i32)
    n = 2 * KP
    sub, lane = grid(n, n, 0), grid(n, n, 1)
    own_t = total(sub == lane, owners, 1)
    earlier = (owners == own_t) & (lane < sub)
    slot_t = own_t * CAP + jnp.sum(earlier.astype(i32), axis=1, keepdims=True)
    sub, lane = grid(n, KP, 0), grid(n, KP, 1)
    which = lax.rem(sub, KP)
    col_n = total(which == lane, columns, 1)
    before = (columns < col_n) | ((columns == col_n) & (lane < which))
    position = 2 * jnp.sum(before.astype(i32), axis=1, keepdims=True)
    position += (grid(n, 1, 0) >= KP).astype(i32)
    taken = slot_t == grid(n, 2 * B, 1)
    inverse = n + total(taken, position - n, 0)
    return order, row_s, col_s, upto, keep, inverse


def fused(
    tokens, hidden, masters, rows, columns, owners, out,
    own, feats, low, high, hidden_raw, hid, table, meta, raw, part, grads,
    part_a, part_b, in_a, in_b, out_a, out_b, in_a2, in_b2, mine, owner_out, owner_in, final_out,
    local_sem, xs, xr, zs, zr, hs, hr, hxs, hxr, ys, yr, cs, cr,
    as_, ar, bs, br, as2, ar2, bs2, br2, os, ors, fs, fr,
):
    x, z, t = place()
    wait_all = greet(
        [x_peer(x, z, t, s) for s in (1, 2, 3)]
        + [z_peer(x, z, t, s) for s in (1, -1, 5, -5)]
        + [y_peer(x, z, t, s) for s in (1, 2, 3)]
        + [core_peer(x, z, t)]
    )
    bring = pltpu.make_async_copy(hidden, hidden_raw, local_sem.at[0])
    bring.start()
    own[...] = masters[...].astype(BF16)
    spot = (z, lax.rem(x, 2), slice(None), pl.ds(pl.multiple_of(x // 2 * B, B), B))
    low[spot] = own[:LOW]
    high[x, z] = own[LOW:]
    for j in range(8):
        feats[t * 8 + j] = tokens[:, j * B : j * B + B]
    my_feats = feats.at[pl.ds(t * 8, 8)]
    wait_all()

    def at_z(offset):
        return lax.rem(z + offset + Z, Z)

    def low_copy(m):
        offset, step = MOVES[m]
        chunk = low.at[at_z(offset)]
        if m in STAGES[3]:
            chunk = low.at[at_z(offset), m - STAGES[3][0]]
        return send(chunk, chunk, zs.at[m], zr.at[m], z_peer(x, z, t, step))

    def high_copy(m):
        offset, step = MOVES[m]
        chunk = high.at[x, at_z(offset)]
        if m in STAGES[3]:
            cut = (B - LOW) // 32 * 16
            rows_m = pl.ds(0, cut) if m == STAGES[3][0] else pl.ds(cut, B - LOW - cut)
            chunk = high.at[x, at_z(offset), rows_m]
        return send(chunk, chunk, hs.at[m], hr.at[m], z_peer(x, z, t, step))

    def high_x(offset, s):
        chunk = high.at[x, at_z(offset)]
        return send(chunk, chunk, hxs.at[offset % Z, s - 1], hxr.at[offset % Z, s - 1], x_peer(x, z, t, s))

    sent = []

    def go(copies):
        for copy in copies:
            copy.start()
            sent.append(copy)

    def spread_x(offsets):
        for offset in offsets:
            go([high_x(offset, s) for s in (1, 3, 2)])

    def arrive(make, stage):
        for m in STAGES[stage]:
            make(m).wait_recv()

    def advance(make, stage):
        go([make(m) for m in STAGES[stage]])

    first = [
        send(own.at[pl.ds(0, LOW)], low.at[spot], xs.at[s - 1], xr.at[s - 1], x_peer(x, z, t, s))
        for s in (1, 3, 2)
    ]
    go(first)
    advance(high_copy, 0)
    y_moves = {
        s: send(my_feats, my_feats, ys.at[s - 1], yr.at[s - 1], y_peer(x, z, t, s))
        for s in (1, 3, 2)
    }
    go(y_moves.values())
    over = send(my_feats, my_feats, cs.at[0], cr.at[0], core_peer(x, z, t))
    go([over])
    spread_x((0,))

    order, row_s, col_s, upto, keep, inverse = tables(rows[...], columns[...], owners[...])
    for r, value in enumerate((order, row_s, col_s, upto, keep)):
        table[r : r + 1, :B] = value
    table[5:6, :] = inverse
    table[6:7, :KP] = rows[...]
    to_scalar = pltpu.make_async_copy(table, meta, local_sem.at[1])
    to_scalar.start()

    for copy in first:
        copy.wait_recv()
    advance(low_copy, 0)
    arrive(high_copy, 0)
    advance(high_copy, 1)
    spread_x((-5, 5, -1, 1))
    bring.wait()
    for c in range(hid.shape[0]):
        hid[c] = hidden_raw[:, c * B : c * B + B]
    arrive(low_copy, 0)
    advance(low_copy, 1)
    arrive(high_copy, 1)
    advance(high_copy, 2)
    spread_x((-6, -4, 4, 6, -2, 2))
    arrive(low_copy, 1)
    advance(low_copy, 2)
    arrive(high_copy, 2)
    advance(high_copy, 3)
    spread_x((-7, 3, -3, 7))

    passed = []
    for s in (1, 3, 2):
        y_moves[s].wait_recv()
        source = feats.at[pl.ds(lax.rem(t - CORES * s + Y * CORES, Y * CORES) * 8, 8)]
        copy = send(source, source, cs.at[s], cr.at[s], core_peer(x, z, t))
        go([copy])
        passed.append(copy)
    arrive(low_copy, 2)
    advance(low_copy, 3)
    arrive(high_copy, 3)
    spread_x((8,))
    to_scalar.wait()
    over.wait_recv()
    for copy in passed:
        copy.wait_recv()

    def forward(offset):
        for s in (1, 3, 2):
            high_x(offset, s).wait_recv()
        zz = at_z(offset)
        for half in range(2):
            spot_k = half * Z + zz
            top = jnp.concatenate([high[half, zz], high[half + 2, zz]], axis=1)
            weight = jnp.concatenate([low[zz, half], top], axis=0)
            raw[spot_k] = jnp.dot(feats[meta[6, spot_k]], weight, preferred_element_type=F32)

    for offset in (0, -5, 5, -1, 1, -6, -4, 4, 6, -2, 2, -7, 3, -3, 7):
        forward(offset)
    arrive(low_copy, 3)
    forward(8)

    part[0] = jnp.zeros_like(part[0])

    @pl.loop(0, KP)
    def _(i):
        part[i + 1] = part[i] * meta[4, i].astype(F32) + raw[meta[0, i]]

    def backward(i, store):
        last = meta[3, i]
        value = part[last]
        gate, up = value[:, :B], value[:, B:]
        upstream = hid[meta[2, i]].astype(F32)
        sig = 1.0 / (1.0 + jnp.exp(-gate))
        scaled = upstream * sig
        grads[:, :B] = (scaled * up * (1.0 + gate * (1.0 - sig))).astype(BF16)
        grads[:, B:] = (scaled * gate).astype(BF16)
        block = lax.dot_general(
            feats[meta[1, i]], grads[...], (((0,), (0,)), ((), ())), preferred_element_type=F32
        )
        for p in range(16):
            r = block[8 * p : 8 * p + 8]
            store(p, jnp.concatenate([r[:, :B], r[:, B:]], axis=0).astype(BF16))

    @pl.loop(0, HALF)
    def _(i):
        at = pl.ds(pl.multiple_of(i * 16, 16), 16)

        def store(p, v):
            part_a[p, at] = v

        backward(i, store)

    def a_copy(j, s):
        piece = lax.rem(x + s, X) * 4 + lax.rem(z + STEPS[j] + Z, 4)
        return send(
            part_a.at[piece], in_a.at[j, s - 1], as_.at[j, s - 1], ar.at[j, s - 1],
            x_peer(x, z, t, s),
        )

    a_copies = [[a_copy(j, s) for s in (1, 3, 2)] for j in range(4)]
    for group in a_copies:
        for copy in group:
            copy.start()

    @pl.loop(0, HALF)
    def _(i):
        at = pl.ds(pl.multiple_of(i * 16, 16), 16)

        def store(p, v):
            part_b[p, at] = v

        backward(i + HALF, store)

    def b_copy(j, k):
        step = STEPS[k] if k or j % 2 == 0 else -STEPS[k]
        piece = lax.rem(x + XSTEPS[j], X) * 4 + lax.rem(z + step + Z, 4)
        return send(
            part_b.at[piece], in_b.at[j, k], bs.at[j, k], br.at[j, k], z_peer(x, z, t, step)
        )

    b_copies = [[b_copy(j, k) for k in (0, 1, 2)] for j in range(4)]
    for group in b_copies:
        for copy in group:
            copy.start()

    tile = 64
    size = HALF * 16

    def merge(own_piece, arrived, store):
        @pl.loop(0, size // tile)
        def _(r):
            at = pl.ds(pl.multiple_of(r * tile, tile), tile)
            value = own_piece[at].astype(F32)
            for k in range(3):
                value += arrived[k, at].astype(F32)
            store(r, at, value)

    second = []
    for j in range(4):
        def keep_a(r, at, value, j=j):
            if j < 3:
                out_a[j, at] = value.astype(BF16)
            else:
                mine[pl.ds(r * 8, 8)] = value.reshape(8, 8, B)

        def keep_b(r, at, value, j=j):
            if j < 3:
                out_b[j, at] = value.astype(BF16)
            else:
                mine[pl.ds(KP + r * 8, 8)] = value.reshape(8, 8, B)

        for copy in a_copies[j]:
            copy.wait_recv()
        merge(part_a.at[x * 4 + lax.rem(z + STEPS[j] + Z, 4)], in_a.at[j], keep_a)
        if j < 3:
            if j == 0:
                cut = size // 2
                pieces = [(pl.ds(0, cut), 0, 2), (pl.ds(cut, cut), 3, -2)]
            else:
                pieces = [(pl.ds(0, size), j, STEPS[j])]
            for at, sem, step in pieces:
                copy = send(out_a.at[j, at], in_a2.at[j, at], as2.at[sem], ar2.at[sem],
                            z_peer(x, z, t, step))
                copy.start()
                second.append(copy)
        for copy in b_copies[j]:
            copy.wait_recv()
        merge(part_b.at[lax.rem(x + XSTEPS[j], X) * 4 + lax.rem(z, 4)], in_b.at[j], keep_b)
        if j < 3:
            copy = send(out_b.at[j], in_b2.at[j], bs2.at[j], br2.at[j], x_peer(x, z, t, XSTEPS[j]))
            copy.start()
            second.append(copy)
    for copy in second:
        copy.wait_recv()

    for base, arrived in ((0, in_a2), (KP, in_b2)):
        @pl.loop(0, size // tile)
        def _(r):
            at = pl.ds(pl.multiple_of(r * tile, tile), tile)
            blocks = pl.ds(base + r * 8, 8)
            value = mine[blocks].reshape(tile, B)
            for j in range(3):
                value += arrived[j, at].astype(F32)
            mine[blocks] = value.reshape(8, 8, B)

    mine[2 * KP] = jnp.zeros((8, B), F32)

    def slot(zo, q):
        return mine[meta[5, (q // CAP * Z + zo) * CAP + q % CAP]]

    owner_copies = []
    for step in (8, 7, 9, 6, 10, 5, 11, 4, 12, 3, 13, 2, 14, 1, 15, 0):
        zo = lax.rem(z + step, Z)
        for q in range(0, 12, 2):
            owner_out[step, 8 * q : 8 * q + 16] = jnp.concatenate(
                [slot(zo, q), slot(zo, q + 1)], axis=0
            ).astype(BF16)
        if step:
            copy = send(owner_out.at[step], owner_in.at[step], os.at[step], ors.at[step],
                        z_peer(x, z, t, step))
            copy.start()
            owner_copies.append(copy)
    for copy in owner_copies:
        copy.wait_recv()
    for e in range(4):
        value = owner_out[0] if e == 0 else owner_in[e]
        value = value.astype(F32)
        for k in (4, 8, 12):
            value += owner_in[e + k].astype(F32)
        row = pl.multiple_of(lax.rem(z - e + Z, 4) * 8, 8)
        for q in range(12):
            final_out[q // CAP, q % CAP, pl.ds(row, 8)] = value[8 * q : 8 * q + 8]
    block_rows = pl.ds(pl.multiple_of(x * 32, 32), 32)
    final = [
        send(final_out.at[lax.rem(x + s, X)], out.at[:, block_rows], fs.at[s - 1], fr.at[s - 1],
             x_peer(x, z, t, s))
        for s in (1, 3, 2)
    ]
    for copy in final:
        copy.start()
    out[:, block_rows] = final_out[x]
    for copy in final:
        copy.wait_recv()
    done = sent + sum(a_copies, []) + sum(b_copies, []) + second + owner_copies + final
    for copy in done:
        copy.wait_send()


def local(tokens, hidden_grad, masters, block_row, block_col, owners):
    size = HALF * 16
    columns = hidden_grad.shape[1] // B
    result = pl.pallas_call(
        fused,
        name="fused",
        out_shape=jax.ShapeDtypeStruct((CAP, B, B), F32),
        in_specs=[VMEM, pl.BlockSpec(memory_space=pl.ANY), VMEM, VMEM, VMEM, VMEM],
        out_specs=VMEM,
        scratch_shapes=[
            pltpu.VMEM((B, B), BF16),
            pltpu.VMEM((Y * CORES * 8, B, B), BF16),
            pltpu.VMEM((Z, 2, LOW, 2 * B), BF16),
            pltpu.VMEM((X, Z, B - LOW, B), BF16),
            pltpu.VMEM(hidden_grad.shape, BF16),
            pltpu.VMEM((columns, B, B), BF16),
            pltpu.VMEM((8, 2 * B), jnp.int32),
            pltpu.SMEM((8, 2 * B), jnp.int32),
            pltpu.VMEM((KP, B, 2 * B), F32),
            pltpu.VMEM((KP + 1, B, 2 * B), F32),
            pltpu.VMEM((B, 2 * B), BF16),
            pltpu.VMEM((16, size, B), BF16),
            pltpu.VMEM((16, size, B), BF16),
            pltpu.VMEM((4, 3, size, B), BF16),
            pltpu.VMEM((4, 3, size, B), BF16),
            pltpu.VMEM((3, size, B), BF16),
            pltpu.VMEM((3, size, B), BF16),
            pltpu.VMEM((3, size, B), BF16),
            pltpu.VMEM((3, size, B), BF16),
            pltpu.VMEM((2 * KP + 1, 8, B), F32),
            pltpu.VMEM((Z, 96, B), BF16),
            pltpu.VMEM((Z, 96, B), BF16),
            pltpu.VMEM((X, CAP, 32, B), F32),
            DMA((2,)),
            DMA((3,)), DMA((3,)), DMA((Z,)), DMA((Z,)), DMA((Z,)), DMA((Z,)), DMA((Z, 3)), DMA((Z, 3)),
            DMA((3,)), DMA((3,)), DMA((4,)), DMA((4,)),
            DMA((4, 3)), DMA((4, 3)), DMA((4, 3)), DMA((4, 3)), DMA((4,)), DMA((4,)), DMA((3,)), DMA((3,)),
            DMA((Z,)), DMA((Z,)), DMA((3,)), DMA((3,)),
        ],
        compiler_params=pltpu.CompilerParams(
            collective_id=0, has_side_effects=True, vmem_limit_bytes=56 << 20
        ),
    )(tokens, hidden_grad, masters.reshape(B, B), block_row, block_col, owners)
    return result[None]


def solution(mesh):
    return jax.shard_map(
        local,
        mesh=mesh,
        in_specs=(
            P("dp", "tensor"),
            P("dp", "tensor"),
            P("tensor", "dp", None, None),
            P("tensor", None),
            P("tensor", None),
            P("tensor", None),
        ),
        out_specs=P("tensor", "dp", None, None),
        check_vma=False,
    )
```

```python
import functools

import jax
import jax.numpy as jnp
from jax import lax
from jax.experimental import pallas as pl
from jax.experimental.pallas import tpu as pltpu
from jax.sharding import PartitionSpec as P

MESH = pl.DeviceIdType.MESH
X, Z, Y, CORES = 4, 16, 4, 2
B = 128
KP = 32
CAP = 3
F32, BF16 = jnp.float32, jnp.bfloat16
VMEM = pl.BlockSpec(memory_space=pltpu.VMEM)
SMEM = pl.BlockSpec(memory_space=pltpu.SMEM)
DMA = pltpu.SemaphoreType.DMA
STEPS = (2, 1, -1, 0)
FAR = (6, 7, 8)
XSTEPS = (2, 1, 3, 0)
FIRST = 18
LOW = 32
MOVES = (
    (0, 5), (0, -5), (0, 1), (0, -1),
    (-5, 1), (-5, -1), (5, 1), (5, -1), (-1, 1), (1, -1),
    (-6, 2), (6, -2), (-6, 1), (4, 1), (-4, -1), (6, -1),
)
STAGES = ((0, 1, 2, 3), (4, 5, 6, 7, 8, 9), (10, 11, 12, 13, 14, 15))
HALVES = (10, 11)


def place():
    dp, t = lax.axis_index("dp"), lax.axis_index("tensor")
    return dp // Z, lax.rem(dp, Z), t


def x_peer(x, z, t, step):
    return (lax.rem(x + step + X, X) * Z + z, t)


def z_peer(x, z, t, step):
    return (x * Z + lax.rem(z + step + Z, Z), t)


def y_peer(x, z, t, step):
    return (x * Z + z, lax.rem(t + CORES * step + Y * CORES, Y * CORES))


def core_peer(x, z, t):
    return (x * Z + z, t + 1 - 2 * lax.rem(t, CORES))


def greet(peers):
    barrier = pltpu.get_barrier_semaphore()
    for peer in peers:
        pl.semaphore_signal(barrier, inc=1, device_id=peer, device_id_type=MESH)
    return lambda: pl.semaphore_wait(barrier, len(peers))


def send(src, dst, send_sem, recv_sem, peer):
    return pltpu.make_async_remote_copy(
        src_ref=src, dst_ref=dst, send_sem=send_sem, recv_sem=recv_sem,
        device_id=peer, device_id_type=MESH,
    )


def total(mask, values, axis):
    return jnp.sum(jnp.where(mask, values, 0), axis=axis, keepdims=True)


def tables(rows, columns, owners):
    i32 = jnp.int32

    def grid(a, b, dim):
        return lax.broadcasted_iota(i32, (a, b), dim)

    sub, lane = grid(KP, KP, 0), grid(KP, KP, 1)
    col_t, row_t = total(sub == lane, columns, 1), total(sub == lane, rows, 1)
    before = (columns < col_t) | ((columns == col_t) & (lane < sub))
    rank_t = jnp.sum(before.astype(i32), axis=1, keepdims=True)
    sub, lane = grid(KP, B, 0), grid(KP, B, 1)
    hit = rank_t == lane
    order = total(hit, sub, 0)
    row_s = total(hit, row_t, 0)
    col_s = total(hit, col_t, 0)
    upto = jnp.sum((col_t <= col_s).astype(i32), axis=0, keepdims=True)
    first = jnp.sum((col_t < col_s).astype(i32), axis=0, keepdims=True)
    keep = (first != lax.broadcasted_iota(i32, (1, B), 1)).astype(i32)
    n = 2 * KP
    sub, lane = grid(n, n, 0), grid(n, n, 1)
    own_t = total(sub == lane, owners, 1)
    earlier = (owners == own_t) & (lane < sub)
    slot_t = own_t * CAP + jnp.sum(earlier.astype(i32), axis=1, keepdims=True)
    sub, lane = grid(n, KP, 0), grid(n, KP, 1)
    which = lax.rem(sub, KP)
    col_n = total(which == lane, columns, 1)
    before = (columns < col_n) | ((columns == col_n) & (lane < which))
    position = 2 * jnp.sum(before.astype(i32), axis=1, keepdims=True)
    position += (grid(n, 1, 0) >= KP).astype(i32)
    taken = slot_t == grid(n, 2 * B, 1)
    inverse = n + total(taken, position - n, 0)
    return order, row_s, col_s, upto, keep, inverse


def fused(
    tokens, hidden, masters, rows, columns, owners, out,
    own, feats, low, high, hidden_raw, hid, table, meta, raw, part,
    part_a, part_b, in_a, in_b, out_a, out_b, in_a2, in_b2, mine, owner_out, owner_in, relay_in, final_out,
    local_sem, xs, xr, zs, zr, hs, hr, hxs, hxr, ys, yr, cs, cr,
    as_, ar, bs, br, as2, ar2, bs2, br2, os, ors, rs, rr, fs, fr,
):
    x, z, t = place()
    wait_all = greet(
        [x_peer(x, z, t, s) for s in (1, 2, 3)]
        + [z_peer(x, z, t, s) for s in (1, -1, 5, -5)]
        + [y_peer(x, z, t, s) for s in (1, 2, 3)]
        + [core_peer(x, z, t)]
    )
    bring = pltpu.make_async_copy(hidden, hidden_raw, local_sem.at[0])
    bring.start()
    own[...] = masters[...].astype(BF16)
    spot = (z, lax.rem(x, 2), slice(None), pl.ds(pl.multiple_of(x // 2 * B, B), B))
    low[spot] = own[:LOW]
    high[x, z] = own[LOW:]
    for j in range(8):
        feats[t * 8 + j] = tokens[:, j * B : j * B + B]
    my_feats = feats.at[pl.ds(t * 8, 8)]
    wait_all()

    def at_z(offset):
        return lax.rem(z + offset + Z, Z)

    def low_copy(m):
        offset, step = MOVES[m]
        chunk = low.at[at_z(offset)]
        if m in HALVES:
            chunk = low.at[at_z(offset), m - HALVES[0]]
        return send(chunk, chunk, zs.at[m], zr.at[m], z_peer(x, z, t, step))

    def high_copy(m):
        offset, step = MOVES[m]
        chunk = high.at[x, at_z(offset)]
        if m in HALVES:
            cut = (B - LOW) // 32 * 16
            rows_m = pl.ds(0, cut) if m == HALVES[0] else pl.ds(cut, B - LOW - cut)
            chunk = high.at[x, at_z(offset), rows_m]
        return send(chunk, chunk, hs.at[m], hr.at[m], z_peer(x, z, t, step))

    def high_x(offset, s):
        chunk = high.at[x, at_z(offset)]
        return send(chunk, chunk, hxs.at[offset % Z, s - 1], hxr.at[offset % Z, s - 1], x_peer(x, z, t, s))

    sent = []

    def go(copies):
        for copy in copies:
            copy.start()
            sent.append(copy)

    def spread_x(offsets):
        for offset in offsets:
            go([high_x(offset, s) for s in (1, 3, 2)])

    def arrive(make, stage):
        for m in STAGES[stage]:
            make(m).wait_recv()

    def advance(make, stage):
        go([make(m) for m in STAGES[stage]])

    first = [
        send(own.at[pl.ds(0, LOW)], low.at[spot], xs.at[s - 1], xr.at[s - 1], x_peer(x, z, t, s))
        for s in (1, 3, 2)
    ]
    go(first)
    advance(high_copy, 0)
    y_moves = {
        s: send(my_feats, my_feats, ys.at[s - 1], yr.at[s - 1], y_peer(x, z, t, s))
        for s in (1, 3, 2)
    }
    go(y_moves.values())
    over = send(my_feats, my_feats, cs.at[0], cr.at[0], core_peer(x, z, t))
    go([over])
    spread_x((0,))

    order, row_s, col_s, upto, keep, inverse = tables(rows[...], columns[...], owners[...])
    for r, value in enumerate((order, row_s, col_s, upto, keep)):
        table[r : r + 1, :B] = value
    table[5:6, :] = inverse
    table[6:7, :KP] = rows[...]
    to_scalar = pltpu.make_async_copy(table, meta, local_sem.at[1])
    to_scalar.start()

    for copy in first:
        copy.wait_recv()
    advance(low_copy, 0)
    arrive(high_copy, 0)
    advance(high_copy, 1)
    spread_x((-5, 5, -1, 1))
    bring.wait()
    for c in range(hid.shape[0]):
        hid[c] = hidden_raw[:, c * B : c * B + B]
    arrive(low_copy, 0)
    advance(low_copy, 1)
    arrive(high_copy, 1)
    advance(high_copy, 2)
    spread_x((-6, -4, 4, 6, -2, 2))
    arrive(low_copy, 1)
    advance(low_copy, 2)
    arrive(high_copy, 2)
    spread_x((-7, 3, -3, 7, 8))

    passed = []
    for s in (1, 3, 2):
        y_moves[s].wait_recv()
        source = feats.at[pl.ds(lax.rem(t - CORES * s + Y * CORES, Y * CORES) * 8, 8)]
        copy = send(source, source, cs.at[s], cr.at[s], core_peer(x, z, t))
        go([copy])
        passed.append(copy)
    to_scalar.wait()
    over.wait_recv()
    for copy in passed:
        copy.wait_recv()

    def forward(offset):
        for s in (1, 3, 2):
            high_x(offset, s).wait_recv()
        zz = at_z(offset)
        for half in range(2):
            spot_k = half * Z + zz
            top = jnp.concatenate([high[half, zz], high[half + 2, zz]], axis=1)
            weight = jnp.concatenate([low[zz, half], top], axis=0)
            raw[spot_k] = jnp.dot(feats[meta[6, spot_k]], weight, preferred_element_type=F32)

    for offset in (0, -5, 5, -1, 1, -6, -4, 4, 6, -2, 2):
        forward(offset)
    arrive(low_copy, 2)
    for offset in (-7, 3, -3, 7):
        forward(offset)
    forward(8)

    part[0] = jnp.zeros_like(part[0])

    @pl.loop(0, KP)
    def _(i):
        part[i + 1] = part[i] * meta[4, i].astype(F32) + raw[meta[0, i]]

    def backward(i, store):
        last = meta[3, i]
        value = part[last]
        gate, up = value[:, :B], value[:, B:]
        upstream = hid[meta[2, i]].astype(F32)
        sig = 1.0 / (1.0 + jnp.exp(-gate))
        scaled = upstream * sig
        grad = jnp.concatenate(
            [(scaled * up * (1.0 + gate * (1.0 - sig))).astype(BF16), (scaled * gate).astype(BF16)], axis=1
        )
        block = lax.dot_general(
            feats[meta[1, i]], grad, (((0,), (0,)), ((), ())), preferred_element_type=F32
        )
        for p in range(16):
            r = block[8 * p : 8 * p + 8]
            store(p, jnp.concatenate([r[:, :B], r[:, B:]], axis=0).astype(BF16))

    @pl.loop(0, FIRST, unroll=2)
    def _(i):
        at = pl.ds(pl.multiple_of(i * 16, 16), 16)

        def store(p, v):
            part_a[p, at] = v

        backward(i, store)

    def a_copy(j, s):
        piece = lax.rem(x + s, X) * 4 + lax.rem(z + STEPS[j] + Z, 4)
        return send(
            part_a.at[piece], in_a.at[j, s - 1], as_.at[j, s - 1], ar.at[j, s - 1],
            x_peer(x, z, t, s),
        )

    a_copies = [[a_copy(j, s) for s in (1, 3, 2)] for j in range(4)]
    for group in a_copies:
        for copy in group:
            copy.start()

    @pl.loop(0, KP - FIRST, unroll=2)
    def _(i):
        at = pl.ds(pl.multiple_of(i * 16, 16), 16)

        def store(p, v):
            part_b[p, at] = v

        backward(i + FIRST, store)

    def b_copy(j, k):
        step = STEPS[k] if k or j % 2 == 0 else -STEPS[k]
        piece = lax.rem(x + XSTEPS[j], X) * 4 + lax.rem(z + step + Z, 4)
        return send(
            part_b.at[piece], in_b.at[j, k], bs.at[j, k], br.at[j, k], z_peer(x, z, t, step)
        )

    b_copies = [[b_copy(j, k) for k in (0, 1, 2)] for j in range(4)]
    for group in b_copies:
        for copy in group:
            copy.start()

    tile = 32

    def merge(count, own_piece, arrived, store):
        @pl.loop(0, count * 16 // tile)
        def _(r):
            at = pl.ds(pl.multiple_of(r * tile, tile), tile)
            value = own_piece[at].astype(F32)
            for k in range(3):
                value += arrived[k, at].astype(F32)
            store(r, at, value)

    second = []
    for j in range(4):
        def keep_a(r, at, value, j=j):
            if j < 3:
                out_a[j, at] = value.astype(BF16)
            else:
                mine[pl.ds(r * 4, 4)] = value.reshape(4, 8, B)

        def keep_b(r, at, value, j=j):
            if j < 3:
                out_b[j, at] = value.astype(BF16)
            else:
                mine[pl.ds(2 * FIRST + r * 4, 4)] = value.reshape(4, 8, B)

        for copy in a_copies[j]:
            copy.wait_recv()
        merge(FIRST, part_a.at[x * 4 + lax.rem(z + STEPS[j] + Z, 4)], in_a.at[j], keep_a)
        if j < 3:
            if j == 0:
                cut = FIRST // 2 * 16
                pieces = [(pl.ds(0, cut), 0, 2), (pl.ds(cut, FIRST * 16 - cut), 3, -2)]
            else:
                pieces = [(pl.ds(0, FIRST * 16), j, STEPS[j])]
            for at, sem, step in pieces:
                copy = send(out_a.at[j, at], in_a2.at[j, at], as2.at[sem], ar2.at[sem],
                            z_peer(x, z, t, step))
                copy.start()
                second.append(copy)
        for copy in b_copies[j]:
            copy.wait_recv()
        merge(KP - FIRST, part_b.at[lax.rem(x + XSTEPS[j], X) * 4 + lax.rem(z, 4)], in_b.at[j], keep_b)
        if j < 3:
            copy = send(out_b.at[j], in_b2.at[j], bs2.at[j], br2.at[j], x_peer(x, z, t, XSTEPS[j]))
            copy.start()
            second.append(copy)
    for copy in second:
        copy.wait_recv()

    for base, count, arrived in ((0, FIRST, in_a2), (2 * FIRST, KP - FIRST, in_b2)):
        @pl.loop(0, count * 16 // tile)
        def _(r):
            at = pl.ds(pl.multiple_of(r * tile, tile), tile)
            blocks = pl.ds(base + r * 4, 4)
            value = mine[blocks].reshape(tile, B)
            for j in range(3):
                value += arrived[j, at].astype(F32)
            mine[blocks] = value.reshape(4, 8, B)

    mine[2 * KP] = jnp.zeros((8, B), F32)

    def slot(zo, q):
        return mine[meta[5, (q // CAP * Z + zo) * CAP + q % CAP]]

    def collect(step):
        zo = lax.rem(z + step + Z, Z)
        for q in range(0, 12, 2):
            owner_out[step % Z, 8 * q : 8 * q + 16] = jnp.concatenate(
                [slot(zo, q), slot(zo, q + 1)], axis=0
            ).astype(BF16)

    half_rows = 48

    def share(step, way):
        if step < 8:
            return pl.ds(0, 96)
        return pl.ds(0 if way > 0 else half_rows, half_rows)

    def relay(step, way):
        k = step - FAR[0] + (0 if way > 0 else len(FAR))
        at = share(step, way)
        return send(owner_out.at[step * way % Z, at], relay_in.at[k, at], rs.at[k], rr.at[k],
                    z_peer(x, z, t, 4 * way))

    def direct(step, way):
        k = step * way % Z
        return send(owner_out.at[k], owner_in.at[k], os.at[k], ors.at[k], z_peer(x, z, t, step * way))

    owner_copies = []
    for step in FAR:
        for way in (1, -1):
            if step < 8 or way > 0:
                collect(step * way)
            copy = relay(step, way)
            copy.start()
            owner_copies.append(copy)
    arrivals = []
    for step in (5, 1):
        for way in (1, -1):
            collect(step * way)
            copy = direct(step, way)
            copy.start()
            arrivals.append(copy)
    for step in (2, 3, 4):
        for way in (1, -1):
            collect(step * way)
    collect(0)
    for step in (2, 3, 4):
        for way in (1, -1):
            relay(step + 4, way).wait_recv()
            at = share(step + 4, way)
            k = step - 2 + (0 if way > 0 else len(FAR))
            near_sum = owner_out[step * way % Z, at].astype(F32) + relay_in[k, at].astype(F32)
            owner_out[step * way % Z, at] = near_sum.astype(BF16)
            copy = direct(step, way)
            copy.start()
            arrivals.append(copy)
    for copy in arrivals:
        copy.wait_recv()
    owner_copies += arrivals
    for e in range(4):
        near = {0: (4, 12), 1: (1, 5, 13), 2: (2, 14), 3: (3, 15, 11)}[e]
        value = owner_out[0].astype(F32) if e == 0 else None
        for k in near:
            more = owner_in[k].astype(F32)
            value = more if value is None else value + more
        row = pl.multiple_of(lax.rem(z - e + Z, 4) * 8, 8)
        for q in range(12):
            final_out[q // CAP, q % CAP, pl.ds(row, 8)] = value[8 * q : 8 * q + 8]
    block_rows = pl.ds(pl.multiple_of(x * 32, 32), 32)
    final = [
        send(final_out.at[lax.rem(x + s, X)], out.at[:, block_rows], fs.at[s - 1], fr.at[s - 1],
             x_peer(x, z, t, s))
        for s in (1, 3, 2)
    ]
    for copy in final:
        copy.start()
    out[:, block_rows] = final_out[x]
    for copy in final:
        copy.wait_recv()
    done = sent + sum(a_copies, []) + sum(b_copies, []) + second + owner_copies + final
    for copy in done:
        copy.wait_send()


def local(tokens, hidden_grad, masters, block_row, block_col, owners):
    size_a, size_b = FIRST * 16, (KP - FIRST) * 16
    columns = hidden_grad.shape[1] // B
    result = pl.pallas_call(
        fused,
        name="fused",
        out_shape=jax.ShapeDtypeStruct((CAP, B, B), F32),
        in_specs=[VMEM, pl.BlockSpec(memory_space=pl.ANY), VMEM, VMEM, VMEM, VMEM],
        out_specs=VMEM,
        scratch_shapes=[
            pltpu.VMEM((B, B), BF16),
            pltpu.VMEM((Y * CORES * 8, B, B), BF16),
            pltpu.VMEM((Z, 2, LOW, 2 * B), BF16),
            pltpu.VMEM((X, Z, B - LOW, B), BF16),
            pltpu.VMEM(hidden_grad.shape, BF16),
            pltpu.VMEM((columns, B, B), BF16),
            pltpu.VMEM((8, 2 * B), jnp.int32),
            pltpu.SMEM((8, 2 * B), jnp.int32),
            pltpu.VMEM((KP, B, 2 * B), F32),
            pltpu.VMEM((KP + 1, B, 2 * B), F32),
            pltpu.VMEM((16, size_a, B), BF16),
            pltpu.VMEM((16, size_b, B), BF16),
            pltpu.VMEM((4, 3, size_a, B), BF16),
            pltpu.VMEM((4, 3, size_b, B), BF16),
            pltpu.VMEM((3, size_a, B), BF16),
            pltpu.VMEM((3, size_b, B), BF16),
            pltpu.VMEM((3, size_a, B), BF16),
            pltpu.VMEM((3, size_b, B), BF16),
            pltpu.VMEM((2 * KP + 1, 8, B), F32),
            pltpu.VMEM((Z, 96, B), BF16),
            pltpu.VMEM((Z, 96, B), BF16),
            pltpu.VMEM((6, 96, B), BF16),
            pltpu.VMEM((X, CAP, 32, B), F32),
            DMA((2,)),
            DMA((3,)), DMA((3,)), DMA((Z,)), DMA((Z,)), DMA((Z,)), DMA((Z,)), DMA((Z, 3)), DMA((Z, 3)),
            DMA((3,)), DMA((3,)), DMA((4,)), DMA((4,)),
            DMA((4, 3)), DMA((4, 3)), DMA((4, 3)), DMA((4, 3)), DMA((4,)), DMA((4,)), DMA((3,)), DMA((3,)),
            DMA((Z,)), DMA((Z,)), DMA((6,)), DMA((6,)), DMA((3,)), DMA((3,)),
        ],
        compiler_params=pltpu.CompilerParams(
            collective_id=0, has_side_effects=True, vmem_limit_bytes=56 << 20
        ),
    )(tokens, hidden_grad, masters.reshape(B, B), block_row, block_col, owners)
    return result[None]


def solution(mesh):
    return jax.shard_map(
        local,
        mesh=mesh,
        in_specs=(
            P("dp", "tensor"),
            P("dp", "tensor"),
            P("tensor", "dp", None, None),
            P("tensor", None),
            P("tensor", None),
            P("tensor", None),
        ),
        out_specs=P("tensor", "dp", None, None),
        check_vma=False,
    )
```

```python
import functools

import jax
import jax.numpy as jnp
from jax import lax
from jax.experimental import pallas as pl
from jax.experimental.pallas import tpu as pltpu
from jax.sharding import PartitionSpec as P

MESH = pl.DeviceIdType.MESH
X, Z, Y, CORES = 4, 16, 4, 2
B = 128
KP = 32
CAP = 3
F32, BF16 = jnp.float32, jnp.bfloat16
VMEM = pl.BlockSpec(memory_space=pltpu.VMEM)
SMEM = pl.BlockSpec(memory_space=pltpu.SMEM)
DMA = pltpu.SemaphoreType.DMA
STEPS = (2, 1, -1, 0)
FAR = (7, 8,)
XSTEPS = (2, 1, 3, 0)
FIRST = 16
LOW = 32
MOVES = (
    (0, 5), (0, -5), (0, 1), (0, -1),
    (-5, 1), (-5, -1), (5, 1), (5, -1), (-1, 1), (1, -1),
    (-6, 2), (6, -2), (-6, 1), (4, 1), (-4, -1), (6, -1),
)
STAGES = ((0, 1, 2, 3), (4, 5, 6, 7, 8, 9), (10, 11, 12, 13, 14, 15))
HALVES = (10, 11)


def place():
    dp, t = lax.axis_index("dp"), lax.axis_index("tensor")
    return dp // Z, lax.rem(dp, Z), t


def x_peer(x, z, t, step):
    return (lax.rem(x + step + X, X) * Z + z, t)


def z_peer(x, z, t, step):
    return (x * Z + lax.rem(z + step + Z, Z), t)


def y_peer(x, z, t, step):
    return (x * Z + z, lax.rem(t + CORES * step + Y * CORES, Y * CORES))


def core_peer(x, z, t):
    return (x * Z + z, t + 1 - 2 * lax.rem(t, CORES))


def greet(peers):
    barrier = pltpu.get_barrier_semaphore()
    for peer in peers:
        pl.semaphore_signal(barrier, inc=1, device_id=peer, device_id_type=MESH)
    return lambda: pl.semaphore_wait(barrier, len(peers))


def send(src, dst, send_sem, recv_sem, peer):
    return pltpu.make_async_remote_copy(
        src_ref=src, dst_ref=dst, send_sem=send_sem, recv_sem=recv_sem,
        device_id=peer, device_id_type=MESH,
    )


def total(mask, values, axis):
    return jnp.sum(jnp.where(mask, values, 0), axis=axis, keepdims=True)


def tables(rows, columns, owners):
    i32 = jnp.int32

    def grid(a, b, dim):
        return lax.broadcasted_iota(i32, (a, b), dim)

    sub, lane = grid(KP, KP, 0), grid(KP, KP, 1)
    col_t, row_t = total(sub == lane, columns, 1), total(sub == lane, rows, 1)
    before = (columns < col_t) | ((columns == col_t) & (lane < sub))
    rank_t = jnp.sum(before.astype(i32), axis=1, keepdims=True)
    sub, lane = grid(KP, B, 0), grid(KP, B, 1)
    hit = rank_t == lane
    order = total(hit, sub, 0)
    row_s = total(hit, row_t, 0)
    col_s = total(hit, col_t, 0)
    upto = jnp.sum((col_t <= col_s).astype(i32), axis=0, keepdims=True)
    first = jnp.sum((col_t < col_s).astype(i32), axis=0, keepdims=True)
    keep = (first != lax.broadcasted_iota(i32, (1, B), 1)).astype(i32)
    n = 2 * KP
    sub, lane = grid(n, n, 0), grid(n, n, 1)
    own_t = total(sub == lane, owners, 1)
    earlier = (owners == own_t) & (lane < sub)
    slot_t = own_t * CAP + jnp.sum(earlier.astype(i32), axis=1, keepdims=True)
    sub, lane = grid(n, KP, 0), grid(n, KP, 1)
    which = lax.rem(sub, KP)
    col_n = total(which == lane, columns, 1)
    before = (columns < col_n) | ((columns == col_n) & (lane < which))
    position = 2 * jnp.sum(before.astype(i32), axis=1, keepdims=True)
    position += (grid(n, 1, 0) >= KP).astype(i32)
    taken = slot_t == grid(n, 2 * B, 1)
    inverse = n + total(taken, position - n, 0)
    return order, row_s, col_s, upto, keep, inverse


def fused(
    tokens, hidden, masters, rows, columns, owners, out,
    own, feats, low, high, hidden_raw, hid, table, meta, raw, part,
    part_a, part_b, in_a, in_b, out_a, out_b, in_a2, in_b2, mine, owner_out, owner_in, relay_in, final_out,
    local_sem, xs, xr, zs, zr, hs, hr, hxs, hxr, ys, yr, cs, cr,
    as_, ar, bs, br, as2, ar2, bs2, br2, os, ors, rs, rr, fs, fr,
):
    x, z, t = place()
    wait_all = greet(
        [x_peer(x, z, t, s) for s in (1, 2, 3)]
        + [z_peer(x, z, t, s) for s in (1, -1, 5, -5)]
        + [y_peer(x, z, t, s) for s in (1, 2, 3)]
        + [core_peer(x, z, t)]
    )
    bring = pltpu.make_async_copy(hidden, hidden_raw, local_sem.at[0])
    bring.start()
    own[...] = masters[...].astype(BF16)
    spot = (z, lax.rem(x, 2), slice(None), pl.ds(pl.multiple_of(x // 2 * B, B), B))
    low[spot] = own[:LOW]
    high[x, z] = own[LOW:]
    for j in range(8):
        feats[t * 8 + j] = tokens[:, j * B : j * B + B]
    my_feats = feats.at[pl.ds(t * 8, 8)]
    wait_all()

    def at_z(offset):
        return lax.rem(z + offset + Z, Z)

    def low_copy(m):
        offset, step = MOVES[m]
        chunk = low.at[at_z(offset)]
        if m in HALVES:
            chunk = low.at[at_z(offset), m - HALVES[0]]
        return send(chunk, chunk, zs.at[m], zr.at[m], z_peer(x, z, t, step))

    def high_copy(m):
        offset, step = MOVES[m]
        chunk = high.at[x, at_z(offset)]
        if m in HALVES:
            cut = (B - LOW) // 32 * 16
            rows_m = pl.ds(0, cut) if m == HALVES[0] else pl.ds(cut, B - LOW - cut)
            chunk = high.at[x, at_z(offset), rows_m]
        return send(chunk, chunk, hs.at[m], hr.at[m], z_peer(x, z, t, step))

    def high_x(offset, s):
        chunk = high.at[x, at_z(offset)]
        return send(chunk, chunk, hxs.at[offset % Z, s - 1], hxr.at[offset % Z, s - 1], x_peer(x, z, t, s))

    sent = []

    def go(copies):
        for copy in copies:
            copy.start()
            sent.append(copy)

    def spread_x(offsets):
        for offset in offsets:
            go([high_x(offset, s) for s in (1, 3, 2)])

    def arrive(make, stage):
        for m in STAGES[stage]:
            make(m).wait_recv()

    def advance(make, stage):
        go([make(m) for m in STAGES[stage]])

    first = [
        send(own.at[pl.ds(0, LOW)], low.at[spot], xs.at[s - 1], xr.at[s - 1], x_peer(x, z, t, s))
        for s in (1, 3, 2)
    ]
    go(first)
    advance(high_copy, 0)
    y_moves = {
        s: send(my_feats, my_feats, ys.at[s - 1], yr.at[s - 1], y_peer(x, z, t, s))
        for s in (1, 3, 2)
    }
    go(y_moves.values())
    over = send(my_feats, my_feats, cs.at[0], cr.at[0], core_peer(x, z, t))
    go([over])
    spread_x((0,))

    order, row_s, col_s, upto, keep, inverse = tables(rows[...], columns[...], owners[...])
    for r, value in enumerate((order, row_s, col_s, upto, keep)):
        table[r : r + 1, :B] = value
    table[5:6, :] = inverse
    table[6:7, :KP] = rows[...]
    to_scalar = pltpu.make_async_copy(table, meta, local_sem.at[1])
    to_scalar.start()

    for copy in first:
        copy.wait_recv()
    advance(low_copy, 0)
    arrive(high_copy, 0)
    advance(high_copy, 1)
    spread_x((-5, 5, -1, 1))
    bring.wait()
    for c in range(hid.shape[0]):
        hid[c] = hidden_raw[:, c * B : c * B + B]
    arrive(low_copy, 0)
    advance(low_copy, 1)
    arrive(high_copy, 1)
    advance(high_copy, 2)
    spread_x((-6, -4, 4, 6, -2, 2))
    arrive(low_copy, 1)
    advance(low_copy, 2)
    arrive(high_copy, 2)
    spread_x((-7, 3, -3, 7, 8))

    passed = []
    for s in (1, 3, 2):
        y_moves[s].wait_recv()
        source = feats.at[pl.ds(lax.rem(t - CORES * s + Y * CORES, Y * CORES) * 8, 8)]
        copy = send(source, source, cs.at[s], cr.at[s], core_peer(x, z, t))
        go([copy])
        passed.append(copy)
    to_scalar.wait()
    over.wait_recv()
    for copy in passed:
        copy.wait_recv()

    def forward(offset):
        for s in (1, 3, 2):
            high_x(offset, s).wait_recv()
        zz = at_z(offset)
        for half in range(2):
            spot_k = half * Z + zz
            top = jnp.concatenate([high[half, zz], high[half + 2, zz]], axis=1)
            weight = jnp.concatenate([low[zz, half], top], axis=0)
            raw[spot_k] = jnp.dot(feats[meta[6, spot_k]], weight, preferred_element_type=F32)

    for offset in (0, -5, 5, -1, 1, -6, -4, 4, 6, -2, 2):
        forward(offset)
    arrive(low_copy, 2)
    for offset in (-7, 3, -3, 7):
        forward(offset)
    forward(8)

    part[0] = jnp.zeros_like(part[0])

    @pl.loop(0, KP, unroll=4)
    def _(i):
        part[i + 1] = part[i] * meta[4, i].astype(F32) + raw[meta[0, i]]

    def backward(i, store):
        last = meta[3, i]
        value = part[last]
        gate, up = value[:, :B], value[:, B:]
        upstream = hid[meta[2, i]].astype(F32)
        sig = 1.0 / (1.0 + jnp.exp(-gate))
        scaled = upstream * sig
        grad = jnp.concatenate(
            [(scaled * up * (1.0 + gate * (1.0 - sig))).astype(BF16), (scaled * gate).astype(BF16)], axis=1
        )
        block = lax.dot_general(
            feats[meta[1, i]], grad, (((0,), (0,)), ((), ())), preferred_element_type=F32
        )
        for p in range(16):
            r = block[8 * p : 8 * p + 8]
            store(p, jnp.concatenate([r[:, :B], r[:, B:]], axis=0).astype(BF16))

    @pl.loop(0, FIRST, unroll=8)
    def _(i):
        at = pl.ds(pl.multiple_of(i * 16, 16), 16)

        def store(p, v):
            part_a[p, at] = v

        backward(i, store)

    def a_copy(j, s):
        piece = lax.rem(x + s, X) * 4 + lax.rem(z + STEPS[j] + Z, 4)
        return send(
            part_a.at[piece], in_a.at[j, s - 1], as_.at[j, s - 1], ar.at[j, s - 1],
            x_peer(x, z, t, s),
        )

    a_copies = [[a_copy(j, s) for s in (1, 3, 2)] for j in range(4)]
    for group in a_copies:
        for copy in group:
            copy.start()

    @pl.loop(0, KP - FIRST, unroll=8)
    def _(i):
        at = pl.ds(pl.multiple_of(i * 16, 16), 16)

        def store(p, v):
            part_b[p, at] = v

        backward(i + FIRST, store)

    def b_copy(j, k):
        step = STEPS[k] if k or j % 2 == 0 else -STEPS[k]
        piece = lax.rem(x + XSTEPS[j], X) * 4 + lax.rem(z + step + Z, 4)
        return send(
            part_b.at[piece], in_b.at[j, k], bs.at[j, k], br.at[j, k], z_peer(x, z, t, step)
        )

    b_copies = [[b_copy(j, k) for k in (0, 1, 2)] for j in range(4)]
    for group in b_copies:
        for copy in group:
            copy.start()

    tile = 32

    def merge(count, own_piece, arrived, store):
        @pl.loop(0, count * 16 // tile)
        def _(r):
            at = pl.ds(pl.multiple_of(r * tile, tile), tile)
            value = own_piece[at].astype(F32)
            for k in range(3):
                value += arrived[k, at].astype(F32)
            store(r, at, value)

    for copy in sent:
        copy.wait_send()
    second = []
    for j in range(4):
        def keep_a(r, at, value, j=j):
            if j < 3:
                out_a[j, at] = value.astype(BF16)
            else:
                mine[pl.ds(r * 4, 4)] = value.reshape(4, 8, B)

        def keep_b(r, at, value, j=j):
            if j < 3:
                out_b[j, at] = value.astype(BF16)
            else:
                mine[pl.ds(2 * FIRST + r * 4, 4)] = value.reshape(4, 8, B)

        for copy in a_copies[j]:
            copy.wait_recv()
        merge(FIRST, part_a.at[x * 4 + lax.rem(z + STEPS[j] + Z, 4)], in_a.at[j], keep_a)
        if j < 3:
            if j == 0:
                cut = FIRST // 2 * 16
                pieces = [(pl.ds(0, cut), 0, 2), (pl.ds(cut, FIRST * 16 - cut), 3, -2)]
            else:
                pieces = [(pl.ds(0, FIRST * 16), j, STEPS[j])]
            for at, sem, step in pieces:
                copy = send(out_a.at[j, at], in_a2.at[j, at], as2.at[sem], ar2.at[sem],
                            z_peer(x, z, t, step))
                copy.start()
                second.append(copy)
        for copy in b_copies[j]:
            copy.wait_recv()
        merge(KP - FIRST, part_b.at[lax.rem(x + XSTEPS[j], X) * 4 + lax.rem(z, 4)], in_b.at[j], keep_b)
        if j < 3:
            copy = send(out_b.at[j], in_b2.at[j], bs2.at[j], br2.at[j], x_peer(x, z, t, XSTEPS[j]))
            copy.start()
            second.append(copy)
    for copy in second:
        copy.wait_recv()

    for base, count, arrived in ((0, FIRST, in_a2), (2 * FIRST, KP - FIRST, in_b2)):
        @pl.loop(0, count * 16 // tile)
        def _(r):
            at = pl.ds(pl.multiple_of(r * tile, tile), tile)
            blocks = pl.ds(base + r * 4, 4)
            value = mine[blocks].reshape(tile, B)
            for j in range(3):
                value += arrived[j, at].astype(F32)
            mine[blocks] = value.reshape(4, 8, B)

    mine[2 * KP] = jnp.zeros((8, B), F32)

    def slot(zo, q):
        return mine[meta[5, (q // CAP * Z + zo) * CAP + q % CAP]]

    def collect(step):
        zo = lax.rem(z + step + Z, Z)
        for q in range(0, 12, 2):
            owner_out[step % Z, 8 * q : 8 * q + 16] = jnp.concatenate(
                [slot(zo, q), slot(zo, q + 1)], axis=0
            ).astype(BF16)

    half_rows = 48

    def share(step, way):
        if step < 8:
            return pl.ds(0, 96)
        return pl.ds(0 if way > 0 else half_rows, half_rows)

    def relay(step, way):
        k = step - FAR[0] + (0 if way > 0 else len(FAR))
        at = share(step, way)
        return send(owner_out.at[step * way % Z, at], relay_in.at[k, at], rs.at[k], rr.at[k],
                    z_peer(x, z, t, 4 * way))

    def direct(step, way):
        k = step * way % Z
        return send(owner_out.at[k], owner_in.at[k], os.at[k], ors.at[k], z_peer(x, z, t, step * way))

    owner_copies = []
    for step in FAR:
        for way in (1, -1):
            if step < 8 or way > 0:
                collect(step * way)
            copy = relay(step, way)
            copy.start()
            owner_copies.append(copy)
    arrivals = []
    for step in (6, 5, 2, 1,):
        for way in (1, -1):
            collect(step * way)
            copy = direct(step, way)
            copy.start()
            arrivals.append(copy)
    for step in (3, 4,):
        for way in (1, -1):
            collect(step * way)
    collect(0)
    for step in (3, 4,):
        for way in (1, -1):
            relay(step + 4, way).wait_recv()
            at = share(step + 4, way)
            k = step - 3 + (0 if way > 0 else len(FAR))
            near_sum = owner_out[step * way % Z, at].astype(F32) + relay_in[k, at].astype(F32)
            owner_out[step * way % Z, at] = near_sum.astype(BF16)
            copy = direct(step, way)
            copy.start()
            arrivals.append(copy)
    for copy in sum(a_copies, []) + sum(b_copies, []) + second:
        copy.wait_send()
    for copy in arrivals:
        copy.wait_recv()
    owner_copies += arrivals
    for e in range(4):
        near = {0: (4, 12), 1: (1, 5, 13), 2: (2, 6, 10, 14), 3: (3, 11, 15)}[e]
        value = owner_out[0].astype(F32) if e == 0 else None
        for k in near:
            more = owner_in[k].astype(F32)
            value = more if value is None else value + more
        row = pl.multiple_of(lax.rem(z - e + Z, 4) * 8, 8)
        for q in range(12):
            final_out[q // CAP, q % CAP, pl.ds(row, 8)] = value[8 * q : 8 * q + 8]
    block_rows = pl.ds(pl.multiple_of(x * 32, 32), 32)
    final = [
        send(final_out.at[lax.rem(x + s, X)], out.at[:, block_rows], fs.at[s - 1], fr.at[s - 1],
             x_peer(x, z, t, s))
        for s in (1, 3, 2)
    ]
    for copy in final:
        copy.start()
    out[:, block_rows] = final_out[x]
    for copy in final:
        copy.wait_recv()
    done = owner_copies + final
    for copy in done:
        copy.wait_send()


def local(tokens, hidden_grad, masters, block_row, block_col, owners):
    size_a, size_b = FIRST * 16, (KP - FIRST) * 16
    columns = hidden_grad.shape[1] // B
    result = pl.pallas_call(
        fused,
        name="fused",
        out_shape=jax.ShapeDtypeStruct((CAP, B, B), F32),
        in_specs=[VMEM, pl.BlockSpec(memory_space=pl.ANY), VMEM, VMEM, VMEM, VMEM],
        out_specs=VMEM,
        scratch_shapes=[
            pltpu.VMEM((B, B), BF16),
            pltpu.VMEM((Y * CORES * 8, B, B), BF16),
            pltpu.VMEM((Z, 2, LOW, 2 * B), BF16),
            pltpu.VMEM((X, Z, B - LOW, B), BF16),
            pltpu.VMEM(hidden_grad.shape, BF16),
            pltpu.VMEM((columns, B, B), BF16),
            pltpu.VMEM((8, 2 * B), jnp.int32),
            pltpu.SMEM((8, 2 * B), jnp.int32),
            pltpu.VMEM((KP, B, 2 * B), F32),
            pltpu.VMEM((KP + 1, B, 2 * B), F32),
            pltpu.VMEM((16, size_a, B), BF16),
            pltpu.VMEM((16, size_b, B), BF16),
            pltpu.VMEM((4, 3, size_a, B), BF16),
            pltpu.VMEM((4, 3, size_b, B), BF16),
            pltpu.VMEM((3, size_a, B), BF16),
            pltpu.VMEM((3, size_b, B), BF16),
            pltpu.VMEM((3, size_a, B), BF16),
            pltpu.VMEM((3, size_b, B), BF16),
            pltpu.VMEM((2 * KP + 1, 8, B), F32),
            pltpu.VMEM((Z, 96, B), BF16),
            pltpu.VMEM((Z, 96, B), BF16),
            pltpu.VMEM((4, 96, B), BF16),
            pltpu.VMEM((X, CAP, 32, B), F32),
            DMA((2,)),
            DMA((3,)), DMA((3,)), DMA((Z,)), DMA((Z,)), DMA((Z,)), DMA((Z,)), DMA((Z, 3)), DMA((Z, 3)),
            DMA((3,)), DMA((3,)), DMA((4,)), DMA((4,)),
            DMA((4, 3)), DMA((4, 3)), DMA((4, 3)), DMA((4, 3)), DMA((4,)), DMA((4,)), DMA((3,)), DMA((3,)),
            DMA((Z,)), DMA((Z,)), DMA((4,)), DMA((4,)), DMA((3,)), DMA((3,)),
        ],
        compiler_params=pltpu.CompilerParams(
            collective_id=0, has_side_effects=True, vmem_limit_bytes=56 << 20
        ),
    )(tokens, hidden_grad, masters.reshape(B, B), block_row, block_col, owners)
    return result[None]


def solution(mesh):
    return jax.shard_map(
        local,
        mesh=mesh,
        in_specs=(
            P("dp", "tensor"),
            P("dp", "tensor"),
            P("tensor", "dp", None, None),
            P("tensor", None),
            P("tensor", None),
            P("tensor", None),
        ),
        out_specs=P("tensor", "dp", None, None),
        check_vma=False,
    )
```

```python
import functools

import jax
import jax.numpy as jnp
from jax import lax
from jax.experimental import pallas as pl
from jax.experimental.pallas import tpu as pltpu
from jax.sharding import PartitionSpec as P

MESH = pl.DeviceIdType.MESH
X, Z, Y, CORES = 4, 16, 4, 2
B = 128
KP = 32
CAP = 3
F32, BF16 = jnp.float32, jnp.bfloat16
VMEM = pl.BlockSpec(memory_space=pltpu.VMEM)
SMEM = pl.BlockSpec(memory_space=pltpu.SMEM)
DMA = pltpu.SemaphoreType.DMA
STEPS = (2, 1, -1, 0)
FAR = (7, 8,)
XSTEPS = (2, 1, 3, 0)
FIRST = 16
LOW = 32
MOVES = (
    (0, 5), (0, -5), (0, 1), (0, -1),
    (-5, 1), (-5, -1), (5, 1), (5, -1), (-1, 1), (1, -1),
    (-6, 2), (6, -2), (-6, 1), (4, 1), (-4, -1), (6, -1),
)
STAGES = ((0, 1, 2, 3), (4, 5, 6, 7, 8, 9), (10, 11, 12, 13, 14, 15))
HALVES = (10, 11)


def place():
    dp, t = lax.axis_index("dp"), lax.axis_index("tensor")
    return dp // Z, lax.rem(dp, Z), t


def x_peer(x, z, t, step):
    return (lax.rem(x + step + X, X) * Z + z, t)


def z_peer(x, z, t, step):
    return (x * Z + lax.rem(z + step + Z, Z), t)


def y_peer(x, z, t, step):
    return (x * Z + z, lax.rem(t + CORES * step + Y * CORES, Y * CORES))


def core_peer(x, z, t):
    return (x * Z + z, t + 1 - 2 * lax.rem(t, CORES))


def greet(peers):
    barrier = pltpu.get_barrier_semaphore()
    for peer in peers:
        pl.semaphore_signal(barrier, inc=1, device_id=peer, device_id_type=MESH)
    return lambda: pl.semaphore_wait(barrier, len(peers))


def send(src, dst, send_sem, recv_sem, peer):
    return pltpu.make_async_remote_copy(
        src_ref=src, dst_ref=dst, send_sem=send_sem, recv_sem=recv_sem,
        device_id=peer, device_id_type=MESH,
    )


def total(mask, values, axis):
    return jnp.sum(jnp.where(mask, values, 0), axis=axis, keepdims=True)


def tables(rows, columns, owners):
    i32 = jnp.int32

    def grid(a, b, dim):
        return lax.broadcasted_iota(i32, (a, b), dim)

    sub, lane = grid(KP, KP, 0), grid(KP, KP, 1)
    col_t, row_t = total(sub == lane, columns, 1), total(sub == lane, rows, 1)
    before = (columns < col_t) | ((columns == col_t) & (lane < sub))
    rank_t = jnp.sum(before.astype(i32), axis=1, keepdims=True)
    sub, lane = grid(KP, B, 0), grid(KP, B, 1)
    hit = rank_t == lane
    order = total(hit, sub, 0)
    row_s = total(hit, row_t, 0)
    col_s = total(hit, col_t, 0)
    upto = jnp.sum((col_t <= col_s).astype(i32), axis=0, keepdims=True)
    first = jnp.sum((col_t < col_s).astype(i32), axis=0, keepdims=True)
    keep = (first != lax.broadcasted_iota(i32, (1, B), 1)).astype(i32)
    n = 2 * KP
    sub, lane = grid(n, n, 0), grid(n, n, 1)
    own_t = total(sub == lane, owners, 1)
    earlier = (owners == own_t) & (lane < sub)
    slot_t = own_t * CAP + jnp.sum(earlier.astype(i32), axis=1, keepdims=True)
    sub, lane = grid(n, KP, 0), grid(n, KP, 1)
    which = lax.rem(sub, KP)
    col_n = total(which == lane, columns, 1)
    before = (columns < col_n) | ((columns == col_n) & (lane < which))
    position = 2 * jnp.sum(before.astype(i32), axis=1, keepdims=True)
    position += (grid(n, 1, 0) >= KP).astype(i32)
    taken = slot_t == grid(n, 2 * B, 1)
    inverse = n + total(taken, position - n, 0)
    return order, row_s, col_s, upto, keep, inverse


def fused(
    tokens, hidden, masters, rows, columns, owners, out,
    own, feats, low, high, hidden_raw, hid, table, meta, raw, part,
    part_a, part_b, in_a, in_b, out_a, out_b, in_a2, in_b2, mine, owner_out, owner_in, relay_in, final_out,
    local_sem, xs, xr, zs, zr, hs, hr, hxs, hxr, ys, yr, cs, cr,
    as_, ar, bs, br, as2, ar2, bs2, br2, os, ors, rs, rr, fs, fr,
):
    x, z, t = place()
    wait_all = greet(
        [x_peer(x, z, t, s) for s in (1, 2, 3)]
        + [z_peer(x, z, t, s) for s in (1, -1, 5, -5)]
        + [y_peer(x, z, t, s) for s in (1, 2, 3)]
        + [core_peer(x, z, t)]
    )
    bring = pltpu.make_async_copy(hidden, hidden_raw, local_sem.at[0])
    bring.start()
    own[...] = masters[...].astype(BF16)
    spot = (z, lax.rem(x, 2), slice(None), pl.ds(pl.multiple_of(x // 2 * B, B), B))
    low[spot] = own[:LOW]
    high[x, z] = own[LOW:]
    for j in range(8):
        feats[t * 8 + j] = tokens[:, j * B : j * B + B]
    my_feats = feats.at[pl.ds(t * 8, 8)]
    wait_all()

    def at_z(offset):
        return lax.rem(z + offset + Z, Z)

    def low_copy(m):
        offset, step = MOVES[m]
        chunk = low.at[at_z(offset)]
        if m in HALVES:
            chunk = low.at[at_z(offset), m - HALVES[0]]
        return send(chunk, chunk, zs.at[m], zr.at[m], z_peer(x, z, t, step))

    def high_copy(m):
        offset, step = MOVES[m]
        chunk = high.at[x, at_z(offset)]
        if m in HALVES:
            cut = (B - LOW) // 32 * 16
            rows_m = pl.ds(0, cut) if m == HALVES[0] else pl.ds(cut, B - LOW - cut)
            chunk = high.at[x, at_z(offset), rows_m]
        return send(chunk, chunk, hs.at[m], hr.at[m], z_peer(x, z, t, step))

    def high_x(offset, s):
        chunk = high.at[x, at_z(offset)]
        return send(chunk, chunk, hxs.at[offset % Z, s - 1], hxr.at[offset % Z, s - 1], x_peer(x, z, t, s))

    sent = []

    def go(copies):
        for copy in copies:
            copy.start()
            sent.append(copy)

    def spread_x(offsets):
        for offset in offsets:
            go([high_x(offset, s) for s in (1, 3, 2)])

    def arrive(make, stage):
        for m in STAGES[stage]:
            make(m).wait_recv()

    def advance(make, stage):
        go([make(m) for m in STAGES[stage]])

    first = [
        send(own.at[pl.ds(0, LOW)], low.at[spot], xs.at[s - 1], xr.at[s - 1], x_peer(x, z, t, s))
        for s in (1, 3, 2)
    ]
    go(first)
    advance(high_copy, 0)
    y_moves = {
        s: send(my_feats, my_feats, ys.at[s - 1], yr.at[s - 1], y_peer(x, z, t, s))
        for s in (1, 3, 2)
    }
    go(y_moves.values())
    over = send(my_feats, my_feats, cs.at[0], cr.at[0], core_peer(x, z, t))
    go([over])
    spread_x((0,))

    order, row_s, col_s, upto, keep, inverse = tables(rows[...], columns[...], owners[...])
    for r, value in enumerate((order, row_s, col_s, upto, keep)):
        table[r : r + 1, :B] = value
    table[5:6, :] = inverse
    table[6:7, :KP] = rows[...]
    to_scalar = pltpu.make_async_copy(table, meta, local_sem.at[1])
    to_scalar.start()

    for copy in first:
        copy.wait_recv()
    advance(low_copy, 0)
    arrive(high_copy, 0)
    advance(high_copy, 1)
    spread_x((-5, 5, -1, 1))
    bring.wait()
    for c in range(hid.shape[0]):
        hid[c] = hidden_raw[:, c * B : c * B + B]
    arrive(low_copy, 0)
    advance(low_copy, 1)
    arrive(high_copy, 1)
    advance(high_copy, 2)
    spread_x((-6, -4, 4, 6, -2, 2))
    arrive(low_copy, 1)
    advance(low_copy, 2)
    arrive(high_copy, 2)
    spread_x((-7, 3, -3, 7, 8))

    passed = []
    for s in (1, 3, 2):
        y_moves[s].wait_recv()
        source = feats.at[pl.ds(lax.rem(t - CORES * s + Y * CORES, Y * CORES) * 8, 8)]
        copy = send(source, source, cs.at[s], cr.at[s], core_peer(x, z, t))
        go([copy])
        passed.append(copy)
    to_scalar.wait()
    over.wait_recv()
    for copy in passed:
        copy.wait_recv()

    def forward(offset):
        for s in (1, 3, 2):
            high_x(offset, s).wait_recv()
        zz = at_z(offset)
        for half in range(2):
            spot_k = half * Z + zz
            top = jnp.concatenate([high[half, zz], high[half + 2, zz]], axis=1)
            weight = jnp.concatenate([low[zz, half], top], axis=0)
            raw[spot_k] = jnp.dot(feats[meta[6, spot_k]], weight, preferred_element_type=F32)

    for offset in (0, -5, 5, -1, 1, -6, -4, 4, 6, -2, 2):
        forward(offset)
    arrive(low_copy, 2)
    for offset in (-7, 3, -3, 7):
        forward(offset)
    forward(8)

    part[0] = jnp.zeros_like(part[0])

    @pl.loop(0, KP, unroll=4)
    def _(i):
        part[i + 1] = part[i] * meta[4, i].astype(F32) + raw[meta[0, i]]

    def backward(i, store):
        last = meta[3, i]
        value = part[last]
        gate, up = value[:, :B], value[:, B:]
        upstream = hid[meta[2, i]].astype(F32)
        sig = 1.0 / (1.0 + jnp.exp(-gate))
        scaled = upstream * sig
        grad = jnp.concatenate(
            [(scaled * up * (1.0 + gate * (1.0 - sig))).astype(BF16), (scaled * gate).astype(BF16)], axis=1
        )
        block = lax.dot_general(
            feats[meta[1, i]], grad, (((0,), (0,)), ((), ())), preferred_element_type=F32
        )
        for p in range(16):
            r = block[8 * p : 8 * p + 8]
            store(p, jnp.concatenate([r[:, :B], r[:, B:]], axis=0).astype(BF16))

    @pl.loop(0, FIRST, unroll=8)
    def _(i):
        at = pl.ds(pl.multiple_of(i * 16, 16), 16)

        def store(p, v):
            part_a[p, at] = v

        backward(i, store)

    def a_copy(j, s):
        piece = lax.rem(x + s, X) * 4 + lax.rem(z + STEPS[j] + Z, 4)
        return send(
            part_a.at[piece], in_a.at[j, s - 1], as_.at[j, s - 1], ar.at[j, s - 1],
            x_peer(x, z, t, s),
        )

    a_copies = [[a_copy(j, s) for s in (1, 3, 2)] for j in range(4)]
    for group in a_copies:
        for copy in group:
            copy.start()

    @pl.loop(0, KP - FIRST, unroll=8)
    def _(i):
        at = pl.ds(pl.multiple_of(i * 16, 16), 16)

        def store(p, v):
            part_b[p, at] = v

        backward(i + FIRST, store)

    def b_copy(j, k):
        step = STEPS[k] if k or j % 2 == 0 else -STEPS[k]
        piece = lax.rem(x + XSTEPS[j], X) * 4 + lax.rem(z + step + Z, 4)
        return send(
            part_b.at[piece], in_b.at[j, k], bs.at[j, k], br.at[j, k], z_peer(x, z, t, step)
        )

    b_copies = [[b_copy(j, k) for k in (0, 1, 2)] for j in range(4)]
    for group in b_copies:
        for copy in group:
            copy.start()

    tile = 32

    def merge(count, own_piece, arrived, store):
        @pl.loop(0, count * 16 // tile)
        def _(r):
            at = pl.ds(pl.multiple_of(r * tile, tile), tile)
            value = own_piece[at].astype(F32)
            for k in range(3):
                value += arrived[k, at].astype(F32)
            store(r, at, value)

    for copy in sent:
        copy.wait_send()
    second = []
    for j in range(4):
        def keep_a(r, at, value, j=j):
            if j < 3:
                out_a[j, at] = value.astype(BF16)
            else:
                mine[pl.ds(r * 4, 4)] = value.reshape(4, 8, B)

        def keep_b(r, at, value, j=j):
            if j < 3:
                out_b[j, at] = value.astype(BF16)
            else:
                mine[pl.ds(2 * FIRST + r * 4, 4)] = value.reshape(4, 8, B)

        for copy in a_copies[j]:
            copy.wait_recv()
        merge(FIRST, part_a.at[x * 4 + lax.rem(z + STEPS[j] + Z, 4)], in_a.at[j], keep_a)
        if j < 3:
            if j == 0:
                cut = FIRST // 2 * 16
                pieces = [(pl.ds(0, cut), 0, 2), (pl.ds(cut, FIRST * 16 - cut), 3, -2)]
            else:
                pieces = [(pl.ds(0, FIRST * 16), j, STEPS[j])]
            for at, sem, step in pieces:
                copy = send(out_a.at[j, at], in_a2.at[j, at], as2.at[sem], ar2.at[sem],
                            z_peer(x, z, t, step))
                copy.start()
                second.append(copy)
        for copy in b_copies[j]:
            copy.wait_recv()
        merge(KP - FIRST, part_b.at[lax.rem(x + XSTEPS[j], X) * 4 + lax.rem(z, 4)], in_b.at[j], keep_b)
        if j < 3:
            copy = send(out_b.at[j], in_b2.at[j], bs2.at[j], br2.at[j], x_peer(x, z, t, XSTEPS[j]))
            copy.start()
            second.append(copy)
    for copy in second:
        copy.wait_recv()

    for base, count, arrived in ((0, FIRST, in_a2), (2 * FIRST, KP - FIRST, in_b2)):
        @pl.loop(0, count * 16 // tile)
        def _(r):
            at = pl.ds(pl.multiple_of(r * tile, tile), tile)
            blocks = pl.ds(base + r * 4, 4)
            value = mine[blocks].reshape(tile, B)
            for j in range(3):
                value += arrived[j, at].astype(F32)
            mine[blocks] = value.reshape(4, 8, B)

    mine[2 * KP] = jnp.zeros((8, B), F32)

    def slot(zo, q):
        return mine[meta[5, (q // CAP * Z + zo) * CAP + q % CAP]]

    def collect(step):
        zo = lax.rem(z + step + Z, Z)
        for q in range(0, 12, 2):
            owner_out[step % Z, 8 * q : 8 * q + 16] = jnp.concatenate(
                [slot(zo, q), slot(zo, q + 1)], axis=0
            ).astype(BF16)

    half_rows = 48

    def share(step, way):
        if step < 8:
            return pl.ds(0, 96)
        return pl.ds(0 if way > 0 else half_rows, half_rows)

    def relay(step, way):
        k = step - FAR[0] + (0 if way > 0 else len(FAR))
        at = share(step, way)
        return send(owner_out.at[step * way % Z, at], relay_in.at[k, at], rs.at[k], rr.at[k],
                    z_peer(x, z, t, 4 * way))

    def direct(step, way):
        k = step * way % Z
        return send(owner_out.at[k], owner_in.at[k], os.at[k], ors.at[k], z_peer(x, z, t, step * way))

    owner_copies = []
    for step in FAR:
        for way in (1, -1):
            if step < 8 or way > 0:
                collect(step * way)
            copy = relay(step, way)
            copy.start()
            owner_copies.append(copy)
    arrivals = []
    for step in (6, 5, 2, 1,):
        for way in (1, -1):
            collect(step * way)
            copy = direct(step, way)
            copy.start()
            arrivals.append(copy)
    for step in (3, 4,):
        for way in (1, -1):
            collect(step * way)
    collect(0)
    for step in (3, 4,):
        for way in (1, -1):
            relay(step + 4, way).wait_recv()
            at = share(step + 4, way)
            k = step - 3 + (0 if way > 0 else len(FAR))
            near_sum = owner_out[step * way % Z, at].astype(F32) + relay_in[k, at].astype(F32)
            owner_out[step * way % Z, at] = near_sum.astype(BF16)
            copy = direct(step, way)
            copy.start()
            arrivals.append(copy)
    for copy in sum(a_copies, []) + sum(b_copies, []) + second:
        copy.wait_send()
    for copy in arrivals:
        copy.wait_recv()
    owner_copies += arrivals
    for e in range(4):
        near = {0: (4, 12), 1: (1, 5, 13), 2: (2, 6, 10, 14), 3: (3, 11, 15)}[e]
        value = owner_out[0].astype(F32) if e == 0 else None
        for k in near:
            more = owner_in[k].astype(F32)
            value = more if value is None else value + more
        row = pl.multiple_of(lax.rem(z - e + Z, 4) * 8, 8)
        for q in range(12):
            final_out[q // CAP, q % CAP, pl.ds(row, 8)] = value[8 * q : 8 * q + 8]
    block_rows = pl.ds(pl.multiple_of(x * 32, 32), 32)
    final = [
        send(final_out.at[lax.rem(x + s, X)], out.at[:, block_rows], fs.at[s - 1], fr.at[s - 1],
             x_peer(x, z, t, s))
        for s in (1, 3, 2)
    ]
    for copy in final:
        copy.start()
    out[:, block_rows] = final_out[x]
    for copy in final:
        copy.wait_recv()
    done = owner_copies + final
    for copy in done:
        copy.wait_send()


def local(tokens, hidden_grad, masters, block_row, block_col, owners):
    size_a, size_b = FIRST * 16, (KP - FIRST) * 16
    columns = hidden_grad.shape[1] // B
    result = pl.pallas_call(
        fused,
        name="fused",
        out_shape=pltpu.VMEM((CAP, B, B), F32),
        in_specs=[VMEM, pl.BlockSpec(memory_space=pl.ANY), VMEM, VMEM, VMEM, VMEM],
        out_specs=VMEM,
        scratch_shapes=[
            pltpu.VMEM((B, B), BF16),
            pltpu.VMEM((Y * CORES * 8, B, B), BF16),
            pltpu.VMEM((Z, 2, LOW, 2 * B), BF16),
            pltpu.VMEM((X, Z, B - LOW, B), BF16),
            pltpu.VMEM(hidden_grad.shape, BF16),
            pltpu.VMEM((columns, B, B), BF16),
            pltpu.VMEM((8, 2 * B), jnp.int32),
            pltpu.SMEM((8, 2 * B), jnp.int32),
            pltpu.VMEM((KP, B, 2 * B), F32),
            pltpu.VMEM((KP + 1, B, 2 * B), F32),
            pltpu.VMEM((16, size_a, B), BF16),
            pltpu.VMEM((16, size_b, B), BF16),
            pltpu.VMEM((4, 3, size_a, B), BF16),
            pltpu.VMEM((4, 3, size_b, B), BF16),
            pltpu.VMEM((3, size_a, B), BF16),
            pltpu.VMEM((3, size_b, B), BF16),
            pltpu.VMEM((3, size_a, B), BF16),
            pltpu.VMEM((3, size_b, B), BF16),
            pltpu.VMEM((2 * KP + 1, 8, B), F32),
            pltpu.VMEM((Z, 96, B), BF16),
            pltpu.VMEM((Z, 96, B), BF16),
            pltpu.VMEM((4, 96, B), BF16),
            pltpu.VMEM((X, CAP, 32, B), F32),
            DMA((2,)),
            DMA((3,)), DMA((3,)), DMA((Z,)), DMA((Z,)), DMA((Z,)), DMA((Z,)), DMA((Z, 3)), DMA((Z, 3)),
            DMA((3,)), DMA((3,)), DMA((4,)), DMA((4,)),
            DMA((4, 3)), DMA((4, 3)), DMA((4, 3)), DMA((4, 3)), DMA((4,)), DMA((4,)), DMA((3,)), DMA((3,)),
            DMA((Z,)), DMA((Z,)), DMA((4,)), DMA((4,)), DMA((3,)), DMA((3,)),
        ],
        compiler_params=pltpu.CompilerParams(
            collective_id=0, has_side_effects=True, vmem_limit_bytes=56 << 20
        ),
    )(tokens, hidden_grad, masters.reshape(B, B), block_row, block_col, owners)
    return result[None]


def solution(mesh):
    return jax.shard_map(
        local,
        mesh=mesh,
        in_specs=(
            P("dp", "tensor"),
            P("dp", "tensor"),
            P("tensor", "dp", None, None),
            P("tensor", None),
            P("tensor", None),
            P("tensor", None),
        ),
        out_specs=P("tensor", "dp", None, None),
        check_vma=False,
    )
```

```python
import functools

import jax
import jax.numpy as jnp
from jax import lax
from jax.experimental import pallas as pl
from jax.experimental.pallas import tpu as pltpu
from jax.sharding import PartitionSpec as P

MESH = pl.DeviceIdType.MESH
X, Z, Y, CORES = 4, 16, 4, 2
B = 128
KP = 32
CAP = 3
F32, BF16 = jnp.float32, jnp.bfloat16
VMEM = pl.BlockSpec(memory_space=pltpu.VMEM)
ANY = pl.BlockSpec(memory_space=pl.ANY)
DMA = pltpu.SemaphoreType.DMA
STEPS = (2, 1, -1, 0)
FAR = (7, 8,)
XSTEPS = (2, 1, 3, 0)
FIRST = 16
LOW = 32
MOVES = (
    (0, 5), (0, -5), (0, 1), (0, -1),
    (-5, 1), (-5, -1), (5, 1), (5, -1), (-1, 1), (1, -1),
    (-6, 2), (6, -2), (-6, 1), (4, 1), (-4, -1), (6, -1),
)
STAGES = ((0, 1, 2, 3), (4, 5, 6, 7, 8, 9), (10, 11, 12, 13, 14, 15))
HALVES = (10, 11)


def place():
    dp, t = lax.axis_index("dp"), lax.axis_index("tensor")
    return dp // Z, lax.rem(dp, Z), t


def x_peer(x, z, t, step):
    return (lax.rem(x + step + X, X) * Z + z, t)


def z_peer(x, z, t, step):
    return (x * Z + lax.rem(z + step + Z, Z), t)


def y_peer(x, z, t, step):
    return (x * Z + z, lax.rem(t + CORES * step + Y * CORES, Y * CORES))


def core_peer(x, z, t):
    return (x * Z + z, t + 1 - 2 * lax.rem(t, CORES))


def greet(peers):
    barrier = pltpu.get_barrier_semaphore()
    for peer in peers:
        pl.semaphore_signal(barrier, inc=1, device_id=peer, device_id_type=MESH)
    return lambda: pl.semaphore_wait(barrier, len(peers))


def send(src, dst, send_sem, recv_sem, peer):
    return pltpu.make_async_remote_copy(
        src_ref=src, dst_ref=dst, send_sem=send_sem, recv_sem=recv_sem,
        device_id=peer, device_id_type=MESH,
    )


def total(mask, values, axis):
    return jnp.sum(jnp.where(mask, values, 0), axis=axis, keepdims=True)


def tables(rows, columns, owners):
    i32 = jnp.int32

    def grid(a, b, dim):
        return lax.broadcasted_iota(i32, (a, b), dim)

    sub, lane = grid(KP, KP, 0), grid(KP, KP, 1)
    col_t, row_t = total(sub == lane, columns, 1), total(sub == lane, rows, 1)
    before = (columns < col_t) | ((columns == col_t) & (lane < sub))
    rank_t = jnp.sum(before.astype(i32), axis=1, keepdims=True)
    sub, lane = grid(KP, B, 0), grid(KP, B, 1)
    hit = rank_t == lane
    order = total(hit, sub, 0)
    row_s = total(hit, row_t, 0)
    col_s = total(hit, col_t, 0)
    upto = jnp.sum((col_t <= col_s).astype(i32), axis=0, keepdims=True)
    first = jnp.sum((col_t < col_s).astype(i32), axis=0, keepdims=True)
    keep = (first != lax.broadcasted_iota(i32, (1, B), 1)).astype(i32)
    n = 2 * KP
    sub, lane = grid(n, n, 0), grid(n, n, 1)
    own_t = total(sub == lane, owners, 1)
    earlier = (owners == own_t) & (lane < sub)
    slot_t = own_t * CAP + jnp.sum(earlier.astype(i32), axis=1, keepdims=True)
    sub, lane = grid(n, KP, 0), grid(n, KP, 1)
    which = lax.rem(sub, KP)
    col_n = total(which == lane, columns, 1)
    before = (columns < col_n) | ((columns == col_n) & (lane < which))
    position = 2 * jnp.sum(before.astype(i32), axis=1, keepdims=True)
    position += (grid(n, 1, 0) >= KP).astype(i32)
    taken = slot_t == grid(n, 2 * B, 1)
    inverse = n + total(taken, position - n, 0)
    return order, row_s, col_s, upto, keep, inverse


def fused(
    tokens, hidden, masters, rows_in, columns_in, owners_in, out,
    rows, columns, owners, own, feats, low, high, masters_raw, tokens_raw, hidden_raw, hid, table, meta, raw, part,
    part_a, part_b, in_a, in_b, out_a, out_b, in_a2, in_b2, mine, owner_out, owner_in, relay_in, final_out,
    local_sem, xs, xr, zs, zr, hs, hr, hxs, hxr, ys, yr, cs, cr,
    as_, ar, bs, br, as2, ar2, bs2, br2, os, ors, rs, rr, fs, fr,
):
    x, z, t = place()
    wait_all = greet(
        [x_peer(x, z, t, s) for s in (1, 2, 3)]
        + [z_peer(x, z, t, s) for s in (1, -1, 5, -5)]
        + [y_peer(x, z, t, s) for s in (1, 2, 3)]
        + [core_peer(x, z, t)]
    )
    bring = pltpu.make_async_copy(hidden, hidden_raw, local_sem.at[0])
    bring_small = [
        pltpu.make_async_copy(source, target, local_sem.at[4 + k])
        for k, (source, target) in enumerate(((rows_in, rows), (columns_in, columns), (owners_in, owners)))
    ]
    bring_masters = pltpu.make_async_copy(masters, masters_raw, local_sem.at[2])
    bring_tokens = pltpu.make_async_copy(tokens, tokens_raw, local_sem.at[3])
    bring_masters.start()
    bring_tokens.start()
    bring.start()
    for copy in bring_small:
        copy.start()
    bring_masters.wait()
    own[...] = masters_raw[...].astype(BF16)
    spot = (z, lax.rem(x, 2), slice(None), pl.ds(pl.multiple_of(x // 2 * B, B), B))
    low[spot] = own[:LOW]
    high[x, z] = own[LOW:]
    bring_tokens.wait()
    for j in range(8):
        feats[t * 8 + j] = tokens_raw[:, j * B : j * B + B]
    my_feats = feats.at[pl.ds(t * 8, 8)]
    wait_all()

    def at_z(offset):
        return lax.rem(z + offset + Z, Z)

    def low_copy(m):
        offset, step = MOVES[m]
        chunk = low.at[at_z(offset)]
        if m in HALVES:
            chunk = low.at[at_z(offset), m - HALVES[0]]
        return send(chunk, chunk, zs.at[m], zr.at[m], z_peer(x, z, t, step))

    def high_copy(m):
        offset, step = MOVES[m]
        chunk = high.at[x, at_z(offset)]
        if m in HALVES:
            cut = (B - LOW) // 32 * 16
            rows_m = pl.ds(0, cut) if m == HALVES[0] else pl.ds(cut, B - LOW - cut)
            chunk = high.at[x, at_z(offset), rows_m]
        return send(chunk, chunk, hs.at[m], hr.at[m], z_peer(x, z, t, step))

    def high_x(offset, s):
        chunk = high.at[x, at_z(offset)]
        return send(chunk, chunk, hxs.at[offset % Z, s - 1], hxr.at[offset % Z, s - 1], x_peer(x, z, t, s))

    sent = []

    def go(copies):
        for copy in copies:
            copy.start()
            sent.append(copy)

    def spread_x(offsets):
        for offset in offsets:
            go([high_x(offset, s) for s in (1, 3, 2)])

    def arrive(make, stage):
        for m in STAGES[stage]:
            make(m).wait_recv()

    def advance(make, stage):
        go([make(m) for m in STAGES[stage]])

    first = [
        send(own.at[pl.ds(0, LOW)], low.at[spot], xs.at[s - 1], xr.at[s - 1], x_peer(x, z, t, s))
        for s in (1, 3, 2)
    ]
    go(first)
    advance(high_copy, 0)
    y_moves = {
        s: send(my_feats, my_feats, ys.at[s - 1], yr.at[s - 1], y_peer(x, z, t, s))
        for s in (1, 3, 2)
    }
    go(y_moves.values())
    over = send(my_feats, my_feats, cs.at[0], cr.at[0], core_peer(x, z, t))
    go([over])
    spread_x((0,))

    for copy in bring_small:
        copy.wait()
    order, row_s, col_s, upto, keep, inverse = tables(rows[...], columns[...], owners[...])
    for r, value in enumerate((order, row_s, col_s, upto, keep)):
        table[r : r + 1, :B] = value
    table[5:6, :] = inverse
    table[6:7, :KP] = rows[...]
    to_scalar = pltpu.make_async_copy(table, meta, local_sem.at[1])
    to_scalar.start()

    for copy in first:
        copy.wait_recv()
    advance(low_copy, 0)
    arrive(high_copy, 0)
    advance(high_copy, 1)
    spread_x((-5, 5, -1, 1))
    bring.wait()
    for c in range(hid.shape[0]):
        hid[c] = hidden_raw[:, c * B : c * B + B]
    arrive(low_copy, 0)
    advance(low_copy, 1)
    arrive(high_copy, 1)
    advance(high_copy, 2)
    spread_x((-6, -4, 4, 6, -2, 2))
    arrive(low_copy, 1)
    advance(low_copy, 2)
    arrive(high_copy, 2)
    spread_x((-7, 3, -3, 7, 8))

    passed = []
    for s in (1, 3, 2):
        y_moves[s].wait_recv()
        source = feats.at[pl.ds(lax.rem(t - CORES * s + Y * CORES, Y * CORES) * 8, 8)]
        copy = send(source, source, cs.at[s], cr.at[s], core_peer(x, z, t))
        go([copy])
        passed.append(copy)
    to_scalar.wait()
    over.wait_recv()
    for copy in passed:
        copy.wait_recv()

    def forward(offset):
        for s in (1, 3, 2):
            high_x(offset, s).wait_recv()
        zz = at_z(offset)
        for half in range(2):
            spot_k = half * Z + zz
            top = jnp.concatenate([high[half, zz], high[half + 2, zz]], axis=1)
            weight = jnp.concatenate([low[zz, half], top], axis=0)
            raw[spot_k] = jnp.dot(feats[meta[6, spot_k]], weight, preferred_element_type=F32)

    for offset in (0, -5, 5, -1, 1, -6, -4, 4, 6, -2, 2):
        forward(offset)
    arrive(low_copy, 2)
    for offset in (-7, 3, -3, 7):
        forward(offset)
    forward(8)

    part[0] = jnp.zeros_like(part[0])

    @pl.loop(0, KP, unroll=4)
    def _(i):
        part[i + 1] = part[i] * meta[4, i].astype(F32) + raw[meta[0, i]]

    def backward(i, store):
        last = meta[3, i]
        value = part[last]
        gate, up = value[:, :B], value[:, B:]
        upstream = hid[meta[2, i]].astype(F32)
        sig = 1.0 / (1.0 + jnp.exp(-gate))
        scaled = upstream * sig
        grad = jnp.concatenate(
            [(scaled * up * (1.0 + gate * (1.0 - sig))).astype(BF16), (scaled * gate).astype(BF16)], axis=1
        )
        block = lax.dot_general(
            feats[meta[1, i]], grad, (((0,), (0,)), ((), ())), preferred_element_type=F32
        )
        for p in range(16):
            r = block[8 * p : 8 * p + 8]
            store(p, jnp.concatenate([r[:, :B], r[:, B:]], axis=0).astype(BF16))

    @pl.loop(0, FIRST, unroll=8)
    def _(i):
        at = pl.ds(pl.multiple_of(i * 16, 16), 16)

        def store(p, v):
            part_a[p, at] = v

        backward(i, store)

    def a_copy(j, s):
        piece = lax.rem(x + s, X) * 4 + lax.rem(z + STEPS[j] + Z, 4)
        return send(
            part_a.at[piece], in_a.at[j, s - 1], as_.at[j, s - 1], ar.at[j, s - 1],
            x_peer(x, z, t, s),
        )

    a_copies = [[a_copy(j, s) for s in (1, 3, 2)] for j in range(4)]
    for group in a_copies:
        for copy in group:
            copy.start()

    @pl.loop(0, KP - FIRST, unroll=8)
    def _(i):
        at = pl.ds(pl.multiple_of(i * 16, 16), 16)

        def store(p, v):
            part_b[p, at] = v

        backward(i + FIRST, store)

    def b_copy(j, k):
        step = STEPS[k] if k or j % 2 == 0 else -STEPS[k]
        piece = lax.rem(x + XSTEPS[j], X) * 4 + lax.rem(z + step + Z, 4)
        return send(
            part_b.at[piece], in_b.at[j, k], bs.at[j, k], br.at[j, k], z_peer(x, z, t, step)
        )

    b_copies = [[b_copy(j, k) for k in (0, 1, 2)] for j in range(4)]
    for group in b_copies:
        for copy in group:
            copy.start()

    tile = 32

    def merge(count, own_piece, arrived, store):
        @pl.loop(0, count * 16 // tile)
        def _(r):
            at = pl.ds(pl.multiple_of(r * tile, tile), tile)
            value = own_piece[at].astype(F32)
            for k in range(3):
                value += arrived[k, at].astype(F32)
            store(r, at, value)

    for copy in sent:
        copy.wait_send()
    second = []
    for j in range(4):
        def keep_a(r, at, value, j=j):
            if j < 3:
                out_a[j, at] = value.astype(BF16)
            else:
                mine[pl.ds(r * 4, 4)] = value.reshape(4, 8, B)

        def keep_b(r, at, value, j=j):
            if j < 3:
                out_b[j, at] = value.astype(BF16)
            else:
                mine[pl.ds(2 * FIRST + r * 4, 4)] = value.reshape(4, 8, B)

        for copy in a_copies[j]:
            copy.wait_recv()
        merge(FIRST, part_a.at[x * 4 + lax.rem(z + STEPS[j] + Z, 4)], in_a.at[j], keep_a)
        if j < 3:
            if j == 0:
                cut = FIRST // 2 * 16
                pieces = [(pl.ds(0, cut), 0, 2), (pl.ds(cut, FIRST * 16 - cut), 3, -2)]
            else:
                pieces = [(pl.ds(0, FIRST * 16), j, STEPS[j])]
            for at, sem, step in pieces:
                copy = send(out_a.at[j, at], in_a2.at[j, at], as2.at[sem], ar2.at[sem],
                            z_peer(x, z, t, step))
                copy.start()
                second.append(copy)
        for copy in b_copies[j]:
            copy.wait_recv()
        merge(KP - FIRST, part_b.at[lax.rem(x + XSTEPS[j], X) * 4 + lax.rem(z, 4)], in_b.at[j], keep_b)
        if j < 3:
            copy = send(out_b.at[j], in_b2.at[j], bs2.at[j], br2.at[j], x_peer(x, z, t, XSTEPS[j]))
            copy.start()
            second.append(copy)
    for copy in second:
        copy.wait_recv()

    for base, count, arrived in ((0, FIRST, in_a2), (2 * FIRST, KP - FIRST, in_b2)):
        @pl.loop(0, count * 16 // tile)
        def _(r):
            at = pl.ds(pl.multiple_of(r * tile, tile), tile)
            blocks = pl.ds(base + r * 4, 4)
            value = mine[blocks].reshape(tile, B)
            for j in range(3):
                value += arrived[j, at].astype(F32)
            mine[blocks] = value.reshape(4, 8, B)

    mine[2 * KP] = jnp.zeros((8, B), F32)

    def slot(zo, q):
        return mine[meta[5, (q // CAP * Z + zo) * CAP + q % CAP]]

    def collect(step):
        zo = lax.rem(z + step + Z, Z)
        for q in range(0, 12, 2):
            owner_out[step % Z, 8 * q : 8 * q + 16] = jnp.concatenate(
                [slot(zo, q), slot(zo, q + 1)], axis=0
            ).astype(BF16)

    half_rows = 48

    def share(step, way):
        if step < 8:
            return pl.ds(0, 96)
        return pl.ds(0 if way > 0 else half_rows, half_rows)

    def relay(step, way):
        k = step - FAR[0] + (0 if way > 0 else len(FAR))
        at = share(step, way)
        return send(owner_out.at[step * way % Z, at], relay_in.at[k, at], rs.at[k], rr.at[k],
                    z_peer(x, z, t, 4 * way))

    def direct(step, way):
        k = step * way % Z
        return send(owner_out.at[k], owner_in.at[k], os.at[k], ors.at[k], z_peer(x, z, t, step * way))

    owner_copies = []
    for step in FAR:
        for way in (1, -1):
            if step < 8 or way > 0:
                collect(step * way)
            copy = relay(step, way)
            copy.start()
            owner_copies.append(copy)
    arrivals = []
    for step in (6, 5, 2, 1,):
        for way in (1, -1):
            collect(step * way)
            copy = direct(step, way)
            copy.start()
            arrivals.append(copy)
    for step in (3, 4,):
        for way in (1, -1):
            collect(step * way)
    collect(0)
    for step in (3, 4,):
        for way in (1, -1):
            relay(step + 4, way).wait_recv()
            at = share(step + 4, way)
            k = step - 3 + (0 if way > 0 else len(FAR))
            near_sum = owner_out[step * way % Z, at].astype(F32) + relay_in[k, at].astype(F32)
            owner_out[step * way % Z, at] = near_sum.astype(BF16)
            copy = direct(step, way)
            copy.start()
            arrivals.append(copy)
    for copy in sum(a_copies, []) + sum(b_copies, []) + second:
        copy.wait_send()
    for copy in arrivals:
        copy.wait_recv()
    owner_copies += arrivals
    for e in range(4):
        near = {0: (4, 12), 1: (1, 5, 13), 2: (2, 6, 10, 14), 3: (3, 11, 15)}[e]
        value = owner_out[0].astype(F32) if e == 0 else None
        for k in near:
            more = owner_in[k].astype(F32)
            value = more if value is None else value + more
        row = pl.multiple_of(lax.rem(z - e + Z, 4) * 8, 8)
        for q in range(12):
            final_out[q // CAP, q % CAP, pl.ds(row, 8)] = value[8 * q : 8 * q + 8]
    block_rows = pl.ds(pl.multiple_of(x * 32, 32), 32)
    final = [
        send(final_out.at[lax.rem(x + s, X)], out.at[:, block_rows], fs.at[s - 1], fr.at[s - 1],
             x_peer(x, z, t, s))
        for s in (1, 3, 2)
    ]
    for copy in final:
        copy.start()
    out[:, block_rows] = final_out[x]
    for copy in final:
        copy.wait_recv()
    done = owner_copies + final
    for copy in done:
        copy.wait_send()


def local(tokens, hidden_grad, masters, block_row, block_col, owners):
    size_a, size_b = FIRST * 16, (KP - FIRST) * 16
    columns = hidden_grad.shape[1] // B
    result = pl.pallas_call(
        fused,
        name="fused",
        out_shape=pltpu.VMEM((CAP, B, B), F32),
        in_specs=[ANY, ANY, ANY, ANY, ANY, ANY],
        out_specs=VMEM,
        scratch_shapes=[
            pltpu.VMEM(block_row.shape, jnp.int32),
            pltpu.VMEM(block_col.shape, jnp.int32),
            pltpu.VMEM(owners.shape, jnp.int32),
            pltpu.VMEM((B, B), BF16),
            pltpu.VMEM((Y * CORES * 8, B, B), BF16),
            pltpu.VMEM((Z, 2, LOW, 2 * B), BF16),
            pltpu.VMEM((X, Z, B - LOW, B), BF16),
            pltpu.VMEM((B, B), F32),
            pltpu.VMEM(tokens.shape, BF16),
            pltpu.VMEM(hidden_grad.shape, BF16),
            pltpu.VMEM((columns, B, B), BF16),
            pltpu.VMEM((8, 2 * B), jnp.int32),
            pltpu.SMEM((8, 2 * B), jnp.int32),
            pltpu.VMEM((KP, B, 2 * B), F32),
            pltpu.VMEM((KP + 1, B, 2 * B), F32),
            pltpu.VMEM((16, size_a, B), BF16),
            pltpu.VMEM((16, size_b, B), BF16),
            pltpu.VMEM((4, 3, size_a, B), BF16),
            pltpu.VMEM((4, 3, size_b, B), BF16),
            pltpu.VMEM((3, size_a, B), BF16),
            pltpu.VMEM((3, size_b, B), BF16),
            pltpu.VMEM((3, size_a, B), BF16),
            pltpu.VMEM((3, size_b, B), BF16),
            pltpu.VMEM((2 * KP + 1, 8, B), F32),
            pltpu.VMEM((Z, 96, B), BF16),
            pltpu.VMEM((Z, 96, B), BF16),
            pltpu.VMEM((4, 96, B), BF16),
            pltpu.VMEM((X, CAP, 32, B), F32),
            DMA((7,)),
            DMA((3,)), DMA((3,)), DMA((Z,)), DMA((Z,)), DMA((Z,)), DMA((Z,)), DMA((Z, 3)), DMA((Z, 3)),
            DMA((3,)), DMA((3,)), DMA((4,)), DMA((4,)),
            DMA((4, 3)), DMA((4, 3)), DMA((4, 3)), DMA((4, 3)), DMA((4,)), DMA((4,)), DMA((3,)), DMA((3,)),
            DMA((Z,)), DMA((Z,)), DMA((4,)), DMA((4,)), DMA((3,)), DMA((3,)),
        ],
        compiler_params=pltpu.CompilerParams(
            collective_id=0, has_side_effects=True, vmem_limit_bytes=56 << 20
        ),
    )(tokens, hidden_grad, masters.reshape(B, B), block_row, block_col, owners)
    return result[None]


def solution(mesh):
    return jax.shard_map(
        local,
        mesh=mesh,
        in_specs=(
            P("dp", "tensor"),
            P("dp", "tensor"),
            P("tensor", "dp", None, None),
            P("tensor", None),
            P("tensor", None),
            P("tensor", None),
        ),
        out_specs=P("tensor", "dp", None, None),
        check_vma=False,
    )
```

```python
import functools

import jax
import jax.numpy as jnp
from jax import lax
from jax.experimental import pallas as pl
from jax.experimental.pallas import tpu as pltpu
from jax.sharding import PartitionSpec as P

MESH = pl.DeviceIdType.MESH
X, Z, Y, CORES = 4, 16, 4, 2
B = 128
KP = 32
CAP = 3
F32, BF16 = jnp.float32, jnp.bfloat16
VMEM = pl.BlockSpec(memory_space=pltpu.VMEM)
ANY = pl.BlockSpec(memory_space=pl.ANY)
DMA = pltpu.SemaphoreType.DMA
STEPS = (2, 1, -1, 0)
FAR = (7, 8,)
XSTEPS = (2, 1, 3, 0)
FIRST = 16
LOW = 32
MOVES = (
    (0, 5), (0, -5), (0, 1), (0, -1),
    (-5, 1), (-5, -1), (5, 1), (5, -1), (-1, 1), (1, -1),
    (-6, 2), (6, -2), (-6, 1), (4, 1), (-4, -1), (6, -1),
)
STAGES = ((0, 1, 2, 3), (4, 5, 6, 7, 8, 9), (10, 11, 12, 13, 14, 15))
HALVES = (10, 11)


def place():
    dp, t = lax.axis_index("dp"), lax.axis_index("tensor")
    return dp // Z, lax.rem(dp, Z), t


def x_peer(x, z, t, step):
    return (lax.rem(x + step + X, X) * Z + z, t)


def z_peer(x, z, t, step):
    return (x * Z + lax.rem(z + step + Z, Z), t)


def y_peer(x, z, t, step):
    return (x * Z + z, lax.rem(t + CORES * step + Y * CORES, Y * CORES))


def core_peer(x, z, t):
    return (x * Z + z, t + 1 - 2 * lax.rem(t, CORES))


def greet(peers):
    barrier = pltpu.get_barrier_semaphore()
    for peer in peers:
        pl.semaphore_signal(barrier, inc=1, device_id=peer, device_id_type=MESH)
    return lambda: pl.semaphore_wait(barrier, len(peers))


def send(src, dst, send_sem, recv_sem, peer):
    return pltpu.make_async_remote_copy(
        src_ref=src, dst_ref=dst, send_sem=send_sem, recv_sem=recv_sem,
        device_id=peer, device_id_type=MESH,
    )


def total(mask, values, axis):
    return jnp.sum(jnp.where(mask, values, 0), axis=axis, keepdims=True)


def tables(rows, columns, owners):
    i32 = jnp.int32

    def grid(a, b, dim):
        return lax.broadcasted_iota(i32, (a, b), dim)

    sub, lane = grid(KP, KP, 0), grid(KP, KP, 1)
    col_t, row_t = total(sub == lane, columns, 1), total(sub == lane, rows, 1)
    before = (columns < col_t) | ((columns == col_t) & (lane < sub))
    rank_t = jnp.sum(before.astype(i32), axis=1, keepdims=True)
    sub, lane = grid(KP, B, 0), grid(KP, B, 1)
    hit = rank_t == lane
    order = total(hit, sub, 0)
    row_s = total(hit, row_t, 0)
    col_s = total(hit, col_t, 0)
    upto = jnp.sum((col_t <= col_s).astype(i32), axis=0, keepdims=True)
    first = jnp.sum((col_t < col_s).astype(i32), axis=0, keepdims=True)
    keep = (first != lax.broadcasted_iota(i32, (1, B), 1)).astype(i32)
    n = 2 * KP
    sub, lane = grid(n, n, 0), grid(n, n, 1)
    own_t = total(sub == lane, owners, 1)
    earlier = (owners == own_t) & (lane < sub)
    slot_t = own_t * CAP + jnp.sum(earlier.astype(i32), axis=1, keepdims=True)
    sub, lane = grid(n, KP, 0), grid(n, KP, 1)
    which = lax.rem(sub, KP)
    col_n = total(which == lane, columns, 1)
    before = (columns < col_n) | ((columns == col_n) & (lane < which))
    position = 2 * jnp.sum(before.astype(i32), axis=1, keepdims=True)
    position += (grid(n, 1, 0) >= KP).astype(i32)
    taken = slot_t == grid(n, 2 * B, 1)
    inverse = n + total(taken, position - n, 0)
    return order, row_s, col_s, upto, keep, inverse


def fused(
    tokens, hidden, masters, rows_in, columns_in, owners_in, out,
    rows, columns, owners, own, feats, low, high, masters_raw, tokens_raw, hidden_raw, hid, table, meta, raw, part,
    part_a, part_b, in_a, in_b, out_a, out_b, in_a2, in_b2, mine, owner_out, owner_in, relay_in, final_out,
    local_sem, xs, xr, zs, zr, hs, hr, hxs, hxr, ys, yr, cs, cr,
    as_, ar, bs, br, as2, ar2, bs2, br2, os, ors, rs, rr, fs, fr,
):
    x, z, t = place()
    wait_all = greet(
        [x_peer(x, z, t, s) for s in (1, 2, 3)]
        + [z_peer(x, z, t, s) for s in (1, -1, 5, -5)]
        + [y_peer(x, z, t, s) for s in (1, 2, 3)]
        + [core_peer(x, z, t)]
    )
    bring = pltpu.make_async_copy(hidden, hidden_raw, local_sem.at[0])
    bring_small = [
        pltpu.make_async_copy(source, target, local_sem.at[4 + k])
        for k, (source, target) in enumerate(((rows_in, rows), (columns_in, columns), (owners_in, owners)))
    ]
    bring_masters = pltpu.make_async_copy(masters, masters_raw, local_sem.at[2])
    bring_tokens = pltpu.make_async_copy(tokens, tokens_raw, local_sem.at[3])
    bring_masters.start()
    bring_tokens.start()
    bring.start()
    for copy in bring_small:
        copy.start()
    bring_masters.wait()
    own[...] = masters_raw[...].astype(BF16)
    spot = (z, lax.rem(x, 2), slice(None), pl.ds(pl.multiple_of(x // 2 * B, B), B))
    low[spot] = own[:LOW]
    high[x, z] = own[LOW:]
    bring_tokens.wait()
    for j in range(8):
        feats[t * 8 + j] = tokens_raw[:, j * B : j * B + B]
    my_feats = feats.at[pl.ds(t * 8, 8)]
    wait_all()

    def at_z(offset):
        return lax.rem(z + offset + Z, Z)

    def low_copy(m):
        offset, step = MOVES[m]
        chunk = low.at[at_z(offset)]
        if m in HALVES:
            chunk = low.at[at_z(offset), m - HALVES[0]]
        return send(chunk, chunk, zs.at[m], zr.at[m], z_peer(x, z, t, step))

    def high_copy(m):
        offset, step = MOVES[m]
        chunk = high.at[x, at_z(offset)]
        if m in HALVES:
            cut = (B - LOW) // 32 * 16
            rows_m = pl.ds(0, cut) if m == HALVES[0] else pl.ds(cut, B - LOW - cut)
            chunk = high.at[x, at_z(offset), rows_m]
        return send(chunk, chunk, hs.at[m], hr.at[m], z_peer(x, z, t, step))

    def high_x(offset, s):
        chunk = high.at[x, at_z(offset)]
        return send(chunk, chunk, hxs.at[offset % Z, s - 1], hxr.at[offset % Z, s - 1], x_peer(x, z, t, s))

    sent = []

    def go(copies):
        for copy in copies:
            copy.start()
            sent.append(copy)

    def spread_x(offsets):
        for offset in offsets:
            go([high_x(offset, s) for s in (1, 3, 2)])

    def arrive(make, stage):
        for m in STAGES[stage]:
            make(m).wait_recv()

    def advance(make, stage):
        go([make(m) for m in STAGES[stage]])

    first = [
        send(own.at[pl.ds(0, LOW)], low.at[spot], xs.at[s - 1], xr.at[s - 1], x_peer(x, z, t, s))
        for s in (1, 3, 2)
    ]
    go(first)
    advance(high_copy, 0)
    y_moves = {
        s: send(my_feats, my_feats, ys.at[s - 1], yr.at[s - 1], y_peer(x, z, t, s))
        for s in (1, 3, 2)
    }
    go(y_moves.values())
    over = send(my_feats, my_feats, cs.at[0], cr.at[0], core_peer(x, z, t))
    go([over])
    spread_x((0,))

    for copy in bring_small:
        copy.wait()
    order, row_s, col_s, upto, keep, inverse = tables(rows[...], columns[...], owners[...])
    for r, value in enumerate((order, row_s, col_s, upto, keep)):
        table[r : r + 1, :B] = value
    table[5:6, :] = inverse
    table[6:7, :KP] = rows[...]
    to_scalar = pltpu.make_async_copy(table, meta, local_sem.at[1])
    to_scalar.start()

    for copy in first:
        copy.wait_recv()
    advance(low_copy, 0)
    arrive(high_copy, 0)
    advance(high_copy, 1)
    spread_x((-5, 5, -1, 1))
    bring.wait()
    for c in range(hid.shape[0]):
        hid[c] = hidden_raw[:, c * B : c * B + B]
    arrive(low_copy, 0)
    advance(low_copy, 1)
    arrive(high_copy, 1)
    advance(high_copy, 2)
    spread_x((-6, -4, 4, 6, -2, 2))
    arrive(low_copy, 1)
    advance(low_copy, 2)
    arrive(high_copy, 2)
    spread_x((-7, 3, -3, 7, 8))

    passed = []
    for s in (1, 3, 2):
        y_moves[s].wait_recv()
        source = feats.at[pl.ds(lax.rem(t - CORES * s + Y * CORES, Y * CORES) * 8, 8)]
        copy = send(source, source, cs.at[s], cr.at[s], core_peer(x, z, t))
        go([copy])
        passed.append(copy)
    to_scalar.wait()
    over.wait_recv()
    for copy in passed:
        copy.wait_recv()

    def forward(offset):
        for s in (1, 3, 2):
            high_x(offset, s).wait_recv()
        zz = at_z(offset)
        for half in range(2):
            spot_k = half * Z + zz
            top = jnp.concatenate([high[half, zz], high[half + 2, zz]], axis=1)
            weight = jnp.concatenate([low[zz, half], top], axis=0)
            raw[spot_k] = jnp.dot(feats[meta[6, spot_k]], weight, preferred_element_type=F32)

    for offset in (0, -5, 5, -1, 1, -6, -4, 4, 6, -2, 2):
        forward(offset)
    arrive(low_copy, 2)
    for offset in (-7, 3, -3, 7):
        forward(offset)
    forward(8)

    part[0] = jnp.zeros_like(part[0])

    @pl.loop(0, KP, unroll=4)
    def _(i):
        part[i + 1] = part[i] * meta[4, i].astype(F32) + raw[meta[0, i]]

    def backward(i, store):
        last = meta[3, i]
        value = part[last]
        gate, up = value[:, :B], value[:, B:]
        upstream = hid[meta[2, i]].astype(F32)
        sig = 1.0 / (1.0 + jnp.exp(-gate))
        scaled = upstream * sig
        grad = jnp.concatenate(
            [(scaled * up * (1.0 + gate * (1.0 - sig))).astype(BF16), (scaled * gate).astype(BF16)], axis=1
        )
        block = lax.dot_general(
            feats[meta[1, i]], grad, (((0,), (0,)), ((), ())), preferred_element_type=F32
        )
        for p in range(16):
            r = block[8 * p : 8 * p + 8]
            store(p, jnp.concatenate([r[:, :B], r[:, B:]], axis=0).astype(BF16))

    @pl.loop(0, FIRST, unroll=16)
    def _(i):
        at = pl.ds(pl.multiple_of(i * 16, 16), 16)

        def store(p, v):
            part_a[p, at] = v

        backward(i, store)

    def a_copy(j, s):
        piece = lax.rem(x + s, X) * 4 + lax.rem(z + STEPS[j] + Z, 4)
        return send(
            part_a.at[piece], in_a.at[j, s - 1], as_.at[j, s - 1], ar.at[j, s - 1],
            x_peer(x, z, t, s),
        )

    a_copies = [[a_copy(j, s) for s in (1, 3, 2)] for j in range(4)]
    for group in a_copies:
        for copy in group:
            copy.start()

    @pl.loop(0, KP - FIRST, unroll=16)
    def _(i):
        at = pl.ds(pl.multiple_of(i * 16, 16), 16)

        def store(p, v):
            part_b[p, at] = v

        backward(i + FIRST, store)

    def b_copy(j, k):
        step = STEPS[k] if k or j % 2 == 0 else -STEPS[k]
        piece = lax.rem(x + XSTEPS[j], X) * 4 + lax.rem(z + step + Z, 4)
        return send(
            part_b.at[piece], in_b.at[j, k], bs.at[j, k], br.at[j, k], z_peer(x, z, t, step)
        )

    b_copies = [[b_copy(j, k) for k in (0, 1, 2)] for j in range(4)]
    for group in b_copies:
        for copy in group:
            copy.start()

    tile = 32

    def merge(count, own_piece, arrived, store):
        @pl.loop(0, count * 16 // tile, unroll=4)
        def _(r):
            at = pl.ds(pl.multiple_of(r * tile, tile), tile)
            value = own_piece[at].astype(F32)
            for k in range(3):
                value += arrived[k, at].astype(F32)
            store(r, at, value)

    for copy in sent:
        copy.wait_send()
    second = []
    for j in range(4):
        def keep_a(r, at, value, j=j):
            if j < 3:
                out_a[j, at] = value.astype(BF16)
            else:
                mine[pl.ds(r * 4, 4)] = value.reshape(4, 8, B)

        def keep_b(r, at, value, j=j):
            if j < 3:
                out_b[j, at] = value.astype(BF16)
            else:
                mine[pl.ds(2 * FIRST + r * 4, 4)] = value.reshape(4, 8, B)

        for copy in a_copies[j]:
            copy.wait_recv()
        merge(FIRST, part_a.at[x * 4 + lax.rem(z + STEPS[j] + Z, 4)], in_a.at[j], keep_a)
        if j < 3:
            if j == 0:
                cut = FIRST // 2 * 16
                pieces = [(pl.ds(0, cut), 0, 2), (pl.ds(cut, FIRST * 16 - cut), 3, -2)]
            else:
                pieces = [(pl.ds(0, FIRST * 16), j, STEPS[j])]
            for at, sem, step in pieces:
                copy = send(out_a.at[j, at], in_a2.at[j, at], as2.at[sem], ar2.at[sem],
                            z_peer(x, z, t, step))
                copy.start()
                second.append(copy)
        for copy in b_copies[j]:
            copy.wait_recv()
        merge(KP - FIRST, part_b.at[lax.rem(x + XSTEPS[j], X) * 4 + lax.rem(z, 4)], in_b.at[j], keep_b)
        if j < 3:
            copy = send(out_b.at[j], in_b2.at[j], bs2.at[j], br2.at[j], x_peer(x, z, t, XSTEPS[j]))
            copy.start()
            second.append(copy)
    for copy in second:
        copy.wait_recv()

    for base, count, arrived in ((0, FIRST, in_a2), (2 * FIRST, KP - FIRST, in_b2)):
        @pl.loop(0, count * 16 // tile, unroll=4)
        def _(r):
            at = pl.ds(pl.multiple_of(r * tile, tile), tile)
            blocks = pl.ds(base + r * 4, 4)
            value = mine[blocks].reshape(tile, B)
            for j in range(3):
                value += arrived[j, at].astype(F32)
            mine[blocks] = value.reshape(4, 8, B)

    mine[2 * KP] = jnp.zeros((8, B), F32)

    def slot(zo, q):
        return mine[meta[5, (q // CAP * Z + zo) * CAP + q % CAP]]

    def collect(step):
        zo = lax.rem(z + step + Z, Z)
        for q in range(0, 12, 2):
            owner_out[step % Z, 8 * q : 8 * q + 16] = jnp.concatenate(
                [slot(zo, q), slot(zo, q + 1)], axis=0
            ).astype(BF16)

    half_rows = 48

    def share(step, way):
        if step < 8:
            return pl.ds(0, 96)
        return pl.ds(0 if way > 0 else half_rows, half_rows)

    def relay(step, way):
        k = step - FAR[0] + (0 if way > 0 else len(FAR))
        at = share(step, way)
        return send(owner_out.at[step * way % Z, at], relay_in.at[k, at], rs.at[k], rr.at[k],
                    z_peer(x, z, t, 4 * way))

    def direct(step, way):
        k = step * way % Z
        return send(owner_out.at[k], owner_in.at[k], os.at[k], ors.at[k], z_peer(x, z, t, step * way))

    owner_copies = []
    for step in FAR:
        for way in (1, -1):
            if step < 8 or way > 0:
                collect(step * way)
            copy = relay(step, way)
            copy.start()
            owner_copies.append(copy)
    arrivals = []
    for step in (6, 5, 2, 1,):
        for way in (1, -1):
            collect(step * way)
            copy = direct(step, way)
            copy.start()
            arrivals.append(copy)
    for step in (3, 4,):
        for way in (1, -1):
            collect(step * way)
    collect(0)
    for step in (3, 4,):
        for way in (1, -1):
            relay(step + 4, way).wait_recv()
            at = share(step + 4, way)
            k = step - 3 + (0 if way > 0 else len(FAR))
            near_sum = owner_out[step * way % Z, at].astype(F32) + relay_in[k, at].astype(F32)
            owner_out[step * way % Z, at] = near_sum.astype(BF16)
            copy = direct(step, way)
            copy.start()
            arrivals.append(copy)
    for copy in sum(a_copies, []) + sum(b_copies, []) + second:
        copy.wait_send()
    for copy in arrivals:
        copy.wait_recv()
    owner_copies += arrivals
    for e in range(4):
        near = {0: (4, 12), 1: (1, 5, 13), 2: (2, 6, 10, 14), 3: (3, 11, 15)}[e]
        value = owner_out[0].astype(F32) if e == 0 else None
        for k in near:
            more = owner_in[k].astype(F32)
            value = more if value is None else value + more
        row = pl.multiple_of(lax.rem(z - e + Z, 4) * 8, 8)
        for q in range(12):
            final_out[q // CAP, q % CAP, pl.ds(row, 8)] = value[8 * q : 8 * q + 8]
    block_rows = pl.ds(pl.multiple_of(x * 32, 32), 32)
    final = [
        send(final_out.at[lax.rem(x + s, X)], out.at[:, block_rows], fs.at[s - 1], fr.at[s - 1],
             x_peer(x, z, t, s))
        for s in (1, 3, 2)
    ]
    for copy in final:
        copy.start()
    out[:, block_rows] = final_out[x]
    for copy in final:
        copy.wait_recv()
    done = owner_copies + final
    for copy in done:
        copy.wait_send()


def local(tokens, hidden_grad, masters, block_row, block_col, owners):
    size_a, size_b = FIRST * 16, (KP - FIRST) * 16
    columns = hidden_grad.shape[1] // B
    result = pl.pallas_call(
        fused,
        name="fused",
        out_shape=pltpu.VMEM((CAP, B, B), F32),
        in_specs=[ANY, ANY, ANY, ANY, ANY, ANY],
        out_specs=VMEM,
        scratch_shapes=[
            pltpu.VMEM(block_row.shape, jnp.int32),
            pltpu.VMEM(block_col.shape, jnp.int32),
            pltpu.VMEM(owners.shape, jnp.int32),
            pltpu.VMEM((B, B), BF16),
            pltpu.VMEM((Y * CORES * 8, B, B), BF16),
            pltpu.VMEM((Z, 2, LOW, 2 * B), BF16),
            pltpu.VMEM((X, Z, B - LOW, B), BF16),
            pltpu.VMEM((B, B), F32),
            pltpu.VMEM(tokens.shape, BF16),
            pltpu.VMEM(hidden_grad.shape, BF16),
            pltpu.VMEM((columns, B, B), BF16),
            pltpu.VMEM((8, 2 * B), jnp.int32),
            pltpu.SMEM((8, 2 * B), jnp.int32),
            pltpu.VMEM((KP, B, 2 * B), F32),
            pltpu.VMEM((KP + 1, B, 2 * B), F32),
            pltpu.VMEM((16, size_a, B), BF16),
            pltpu.VMEM((16, size_b, B), BF16),
            pltpu.VMEM((4, 3, size_a, B), BF16),
            pltpu.VMEM((4, 3, size_b, B), BF16),
            pltpu.VMEM((3, size_a, B), BF16),
            pltpu.VMEM((3, size_b, B), BF16),
            pltpu.VMEM((3, size_a, B), BF16),
            pltpu.VMEM((3, size_b, B), BF16),
            pltpu.VMEM((2 * KP + 1, 8, B), F32),
            pltpu.VMEM((Z, 96, B), BF16),
            pltpu.VMEM((Z, 96, B), BF16),
            pltpu.VMEM((4, 96, B), BF16),
            pltpu.VMEM((X, CAP, 32, B), F32),
            DMA((7,)),
            DMA((3,)), DMA((3,)), DMA((Z,)), DMA((Z,)), DMA((Z,)), DMA((Z,)), DMA((Z, 3)), DMA((Z, 3)),
            DMA((3,)), DMA((3,)), DMA((4,)), DMA((4,)),
            DMA((4, 3)), DMA((4, 3)), DMA((4, 3)), DMA((4, 3)), DMA((4,)), DMA((4,)), DMA((3,)), DMA((3,)),
            DMA((Z,)), DMA((Z,)), DMA((4,)), DMA((4,)), DMA((3,)), DMA((3,)),
        ],
        compiler_params=pltpu.CompilerParams(
            collective_id=0, has_side_effects=True, vmem_limit_bytes=56 << 20
        ),
    )(tokens, hidden_grad, masters.reshape(B, B), block_row, block_col, owners)
    return result[None]


def solution(mesh):
    return jax.shard_map(
        local,
        mesh=mesh,
        in_specs=(
            P("dp", "tensor"),
            P("dp", "tensor"),
            P("tensor", "dp", None, None),
            P("tensor", None),
            P("tensor", None),
            P("tensor", None),
        ),
        out_specs=P("tensor", "dp", None, None),
        check_vma=False,
    )
```

```python
import functools

import jax
import jax.numpy as jnp
from jax import lax
from jax.experimental import pallas as pl
from jax.experimental.pallas import tpu as pltpu
from jax.sharding import PartitionSpec as P

MESH = pl.DeviceIdType.MESH
X, Z, Y, CORES = 4, 16, 4, 2
B = 128
KP = 32
CAP = 3
F32, BF16 = jnp.float32, jnp.bfloat16
VMEM = pl.BlockSpec(memory_space=pltpu.VMEM)
ANY = pl.BlockSpec(memory_space=pl.ANY)
DMA = pltpu.SemaphoreType.DMA
STEPS = (2, 1, -1, 0)
FAR = (7, 8,)
XSTEPS = (2, 1, 3, 0)
FIRST = 16
LOW = 32
MOVES = (
    (0, 5), (0, -5), (0, 1), (0, -1),
    (-5, 1), (-5, -1), (5, 1), (5, -1), (-1, 1), (1, -1),
    (-6, 2), (6, -2), (-6, 1), (4, 1), (-4, -1), (6, -1),
)
STAGES = ((0, 1, 2, 3), (4, 5, 6, 7, 8, 9), (10, 11, 12, 13, 14, 15))
HALVES = (10, 11)


def place():
    dp, t = lax.axis_index("dp"), lax.axis_index("tensor")
    return dp // Z, lax.rem(dp, Z), t


def x_peer(x, z, t, step):
    return (lax.rem(x + step + X, X) * Z + z, t)


def z_peer(x, z, t, step):
    return (x * Z + lax.rem(z + step + Z, Z), t)


def y_peer(x, z, t, step):
    return (x * Z + z, lax.rem(t + CORES * step + Y * CORES, Y * CORES))


def core_peer(x, z, t):
    return (x * Z + z, t + 1 - 2 * lax.rem(t, CORES))


def greet(peers):
    barrier = pltpu.get_barrier_semaphore()
    for peer in peers:
        pl.semaphore_signal(barrier, inc=1, device_id=peer, device_id_type=MESH)
    return lambda: pl.semaphore_wait(barrier, len(peers))


def send(src, dst, send_sem, recv_sem, peer):
    return pltpu.make_async_remote_copy(
        src_ref=src, dst_ref=dst, send_sem=send_sem, recv_sem=recv_sem,
        device_id=peer, device_id_type=MESH,
    )


def total(mask, values, axis):
    return jnp.sum(jnp.where(mask, values, 0), axis=axis, keepdims=True)


def tables(rows, columns, owners):
    i32 = jnp.int32

    def grid(a, b, dim):
        return lax.broadcasted_iota(i32, (a, b), dim)

    sub, lane = grid(KP, KP, 0), grid(KP, KP, 1)
    col_t, row_t = total(sub == lane, columns, 1), total(sub == lane, rows, 1)
    before = (columns < col_t) | ((columns == col_t) & (lane < sub))
    rank_t = jnp.sum(before.astype(i32), axis=1, keepdims=True)
    sub, lane = grid(KP, B, 0), grid(KP, B, 1)
    hit = rank_t == lane
    order = total(hit, sub, 0)
    row_s = total(hit, row_t, 0)
    col_s = total(hit, col_t, 0)
    upto = jnp.sum((col_t <= col_s).astype(i32), axis=0, keepdims=True)
    first = jnp.sum((col_t < col_s).astype(i32), axis=0, keepdims=True)
    keep = (first != lax.broadcasted_iota(i32, (1, B), 1)).astype(i32)
    n = 2 * KP
    sub, lane = grid(n, n, 0), grid(n, n, 1)
    own_t = total(sub == lane, owners, 1)
    earlier = (owners == own_t) & (lane < sub)
    slot_t = own_t * CAP + jnp.sum(earlier.astype(i32), axis=1, keepdims=True)
    sub, lane = grid(n, KP, 0), grid(n, KP, 1)
    which = lax.rem(sub, KP)
    col_n = total(which == lane, columns, 1)
    before = (columns < col_n) | ((columns == col_n) & (lane < which))
    position = 2 * jnp.sum(before.astype(i32), axis=1, keepdims=True)
    position += (grid(n, 1, 0) >= KP).astype(i32)
    taken = slot_t == grid(n, 2 * B, 1)
    inverse = n + total(taken, position - n, 0)
    return order, row_s, col_s, upto, keep, inverse


def fused(
    tokens, hidden, masters, rows_in, columns_in, owners_in, out,
    rows, columns, owners, own, feats, low, high, masters_raw, tokens_raw, hidden_raw, hid, table, meta, raw, part,
    part_a, part_b, in_a, in_b, out_a, out_b, in_a2, in_b2, mine, owner_out, owner_in, relay_in, final_out,
    local_sem, xs, xr, zs, zr, hs, hr, hxs, hxr, ys, yr, cs, cr,
    as_, ar, bs, br, as2, ar2, bs2, br2, os, ors, rs, rr, fs, fr,
):
    x, z, t = place()
    wait_all = greet(
        [x_peer(x, z, t, s) for s in (1, 2, 3)]
        + [z_peer(x, z, t, s) for s in (1, -1, 5, -5)]
        + [y_peer(x, z, t, s) for s in (1, 2, 3)]
        + [core_peer(x, z, t)]
    )
    bring = pltpu.make_async_copy(hidden, hidden_raw, local_sem.at[0])
    bring_small = [
        pltpu.make_async_copy(source, target, local_sem.at[4 + k])
        for k, (source, target) in enumerate(((rows_in, rows), (columns_in, columns), (owners_in, owners)))
    ]
    bring_masters = pltpu.make_async_copy(masters, masters_raw, local_sem.at[2])
    bring_tokens = pltpu.make_async_copy(tokens, tokens_raw, local_sem.at[3])
    bring_masters.start()
    bring_tokens.start()
    bring.start()
    for copy in bring_small:
        copy.start()
    bring_masters.wait()
    own[...] = masters_raw[...].astype(BF16)
    spot = (z, lax.rem(x, 2), slice(None), pl.ds(pl.multiple_of(x // 2 * B, B), B))
    low[spot] = own[:LOW]
    high[x, z] = own[LOW:]
    bring_tokens.wait()
    for j in range(8):
        feats[t * 8 + j] = tokens_raw[:, j * B : j * B + B]
    my_feats = feats.at[pl.ds(t * 8, 8)]
    wait_all()

    def at_z(offset):
        return lax.rem(z + offset + Z, Z)

    def low_copy(m):
        offset, step = MOVES[m]
        chunk = low.at[at_z(offset)]
        if m in HALVES:
            chunk = low.at[at_z(offset), m - HALVES[0]]
        return send(chunk, chunk, zs.at[m], zr.at[m], z_peer(x, z, t, step))

    def high_copy(m):
        offset, step = MOVES[m]
        chunk = high.at[x, at_z(offset)]
        if m in HALVES:
            cut = (B - LOW) // 32 * 16
            rows_m = pl.ds(0, cut) if m == HALVES[0] else pl.ds(cut, B - LOW - cut)
            chunk = high.at[x, at_z(offset), rows_m]
        return send(chunk, chunk, hs.at[m], hr.at[m], z_peer(x, z, t, step))

    def high_x(offset, s):
        chunk = high.at[x, at_z(offset)]
        return send(chunk, chunk, hxs.at[offset % Z, s - 1], hxr.at[offset % Z, s - 1], x_peer(x, z, t, s))

    sent = []

    def go(copies):
        for copy in copies:
            copy.start()
            sent.append(copy)

    def spread_x(offsets):
        for offset in offsets:
            go([high_x(offset, s) for s in (1, 3, 2)])

    def arrive(make, stage):
        for m in STAGES[stage]:
            make(m).wait_recv()

    def advance(make, stage):
        go([make(m) for m in STAGES[stage]])

    first = [
        send(own.at[pl.ds(0, LOW)], low.at[spot], xs.at[s - 1], xr.at[s - 1], x_peer(x, z, t, s))
        for s in (1, 3, 2)
    ]
    go(first)
    advance(high_copy, 0)
    y_moves = {
        s: send(my_feats, my_feats, ys.at[s - 1], yr.at[s - 1], y_peer(x, z, t, s))
        for s in (1, 3, 2)
    }
    go(y_moves.values())
    over = send(my_feats, my_feats, cs.at[0], cr.at[0], core_peer(x, z, t))
    go([over])
    spread_x((0,))

    for copy in bring_small:
        copy.wait()
    order, row_s, col_s, upto, keep, inverse = tables(rows[...], columns[...], owners[...])
    for r, value in enumerate((order, row_s, col_s, upto, keep)):
        table[r : r + 1, :B] = value
    table[5:6, :] = inverse
    table[6:7, :KP] = rows[...]
    to_scalar = pltpu.make_async_copy(table, meta, local_sem.at[1])
    to_scalar.start()

    for copy in first:
        copy.wait_recv()
    advance(low_copy, 0)
    arrive(high_copy, 0)
    advance(high_copy, 1)
    spread_x((-5, 5, -1, 1))
    bring.wait()
    for c in range(hid.shape[0]):
        hid[c] = hidden_raw[:, c * B : c * B + B]
    arrive(low_copy, 0)
    advance(low_copy, 1)
    arrive(high_copy, 1)
    advance(high_copy, 2)
    spread_x((-6, -4, 4, 6, -2, 2))
    arrive(low_copy, 1)
    advance(low_copy, 2)
    arrive(high_copy, 2)
    spread_x((-7, 3, -3, 7, 8))

    passed = []
    for s in (1, 3, 2):
        y_moves[s].wait_recv()
        source = feats.at[pl.ds(lax.rem(t - CORES * s + Y * CORES, Y * CORES) * 8, 8)]
        copy = send(source, source, cs.at[s], cr.at[s], core_peer(x, z, t))
        go([copy])
        passed.append(copy)
    to_scalar.wait()
    over.wait_recv()
    for copy in passed:
        copy.wait_recv()

    def forward(offset):
        for s in (1, 3, 2):
            high_x(offset, s).wait_recv()
        zz = at_z(offset)
        for half in range(2):
            spot_k = half * Z + zz
            top = jnp.concatenate([high[half, zz], high[half + 2, zz]], axis=1)
            weight = jnp.concatenate([low[zz, half], top], axis=0)
            raw[spot_k] = jnp.dot(feats[meta[6, spot_k]], weight, preferred_element_type=F32)

    for offset in (0, -5, 5, -1, 1, -6, -4, 4, 6, -2, 2):
        forward(offset)
    arrive(low_copy, 2)
    for offset in (-7, 3, -3, 7):
        forward(offset)
    forward(8)

    part[0] = jnp.zeros_like(part[0])

    @pl.loop(0, KP, unroll=16)
    def _(i):
        part[i + 1] = part[i] * meta[4, i].astype(F32) + raw[meta[0, i]]

    def backward(i, store):
        last = meta[3, i]
        value = part[last]
        gate, up = value[:, :B], value[:, B:]
        upstream = hid[meta[2, i]].astype(F32)
        sig = 1.0 / (1.0 + jnp.exp(-gate))
        scaled = upstream * sig
        grad = jnp.concatenate(
            [(scaled * up * (1.0 + gate * (1.0 - sig))).astype(BF16), (scaled * gate).astype(BF16)], axis=1
        )
        block = lax.dot_general(
            feats[meta[1, i]], grad, (((0,), (0,)), ((), ())), preferred_element_type=F32
        )
        for p in range(16):
            r = block[8 * p : 8 * p + 8]
            store(p, jnp.concatenate([r[:, :B], r[:, B:]], axis=0).astype(BF16))

    @pl.loop(0, FIRST, unroll=16)
    def _(i):
        at = pl.ds(pl.multiple_of(i * 16, 16), 16)

        def store(p, v):
            part_a[p, at] = v

        backward(i, store)

    def a_copy(j, s):
        piece = lax.rem(x + s, X) * 4 + lax.rem(z + STEPS[j] + Z, 4)
        return send(
            part_a.at[piece], in_a.at[j, s - 1], as_.at[j, s - 1], ar.at[j, s - 1],
            x_peer(x, z, t, s),
        )

    a_copies = [[a_copy(j, s) for s in (1, 3, 2)] for j in range(4)]
    for group in a_copies:
        for copy in group:
            copy.start()

    @pl.loop(0, KP - FIRST, unroll=16)
    def _(i):
        at = pl.ds(pl.multiple_of(i * 16, 16), 16)

        def store(p, v):
            part_b[p, at] = v

        backward(i + FIRST, store)

    def b_copy(j, k):
        step = STEPS[k] if k or j % 2 == 0 else -STEPS[k]
        piece = lax.rem(x + XSTEPS[j], X) * 4 + lax.rem(z + step + Z, 4)
        return send(
            part_b.at[piece], in_b.at[j, k], bs.at[j, k], br.at[j, k], z_peer(x, z, t, step)
        )

    b_copies = [[b_copy(j, k) for k in (0, 1, 2)] for j in range(4)]
    for group in b_copies:
        for copy in group:
            copy.start()

    tile = 32

    def merge(count, own_piece, arrived, store):
        @pl.loop(0, count * 16 // tile, unroll=8)
        def _(r):
            at = pl.ds(pl.multiple_of(r * tile, tile), tile)
            value = own_piece[at].astype(F32)
            for k in range(3):
                value += arrived[k, at].astype(F32)
            store(r, at, value)

    for copy in sent:
        copy.wait_send()
    second = []
    for j in range(4):
        def keep_a(r, at, value, j=j):
            if j < 3:
                out_a[j, at] = value.astype(BF16)
            else:
                mine[pl.ds(r * 4, 4)] = value.reshape(4, 8, B)

        def keep_b(r, at, value, j=j):
            if j < 3:
                out_b[j, at] = value.astype(BF16)
            else:
                mine[pl.ds(2 * FIRST + r * 4, 4)] = value.reshape(4, 8, B)

        for copy in a_copies[j]:
            copy.wait_recv()
        merge(FIRST, part_a.at[x * 4 + lax.rem(z + STEPS[j] + Z, 4)], in_a.at[j], keep_a)
        if j < 3:
            if j == 0:
                cut = FIRST // 2 * 16
                pieces = [(pl.ds(0, cut), 0, 2), (pl.ds(cut, FIRST * 16 - cut), 3, -2)]
            else:
                pieces = [(pl.ds(0, FIRST * 16), j, STEPS[j])]
            for at, sem, step in pieces:
                copy = send(out_a.at[j, at], in_a2.at[j, at], as2.at[sem], ar2.at[sem],
                            z_peer(x, z, t, step))
                copy.start()
                second.append(copy)
        for copy in b_copies[j]:
            copy.wait_recv()
        merge(KP - FIRST, part_b.at[lax.rem(x + XSTEPS[j], X) * 4 + lax.rem(z, 4)], in_b.at[j], keep_b)
        if j < 3:
            copy = send(out_b.at[j], in_b2.at[j], bs2.at[j], br2.at[j], x_peer(x, z, t, XSTEPS[j]))
            copy.start()
            second.append(copy)
    for copy in second:
        copy.wait_recv()

    for base, count, arrived in ((0, FIRST, in_a2), (2 * FIRST, KP - FIRST, in_b2)):
        @pl.loop(0, count * 16 // tile, unroll=8)
        def _(r):
            at = pl.ds(pl.multiple_of(r * tile, tile), tile)
            blocks = pl.ds(base + r * 4, 4)
            value = mine[blocks].reshape(tile, B)
            for j in range(3):
                value += arrived[j, at].astype(F32)
            mine[blocks] = value.reshape(4, 8, B)

    mine[2 * KP] = jnp.zeros((8, B), F32)

    def slot(zo, q):
        return mine[meta[5, (q // CAP * Z + zo) * CAP + q % CAP]]

    def collect(step):
        zo = lax.rem(z + step + Z, Z)
        for q in range(0, 12, 2):
            owner_out[step % Z, 8 * q : 8 * q + 16] = jnp.concatenate(
                [slot(zo, q), slot(zo, q + 1)], axis=0
            ).astype(BF16)

    half_rows = 48

    def share(step, way):
        if step < 8:
            return pl.ds(0, 96)
        return pl.ds(0 if way > 0 else half_rows, half_rows)

    def relay(step, way):
        k = step - FAR[0] + (0 if way > 0 else len(FAR))
        at = share(step, way)
        return send(owner_out.at[step * way % Z, at], relay_in.at[k, at], rs.at[k], rr.at[k],
                    z_peer(x, z, t, 4 * way))

    def direct(step, way):
        k = step * way % Z
        return send(owner_out.at[k], owner_in.at[k], os.at[k], ors.at[k], z_peer(x, z, t, step * way))

    owner_copies = []
    for step in FAR:
        for way in (1, -1):
            if step < 8 or way > 0:
                collect(step * way)
            copy = relay(step, way)
            copy.start()
            owner_copies.append(copy)
    arrivals = []
    for step in (6, 5, 2, 1,):
        for way in (1, -1):
            collect(step * way)
            copy = direct(step, way)
            copy.start()
            arrivals.append(copy)
    for step in (3, 4,):
        for way in (1, -1):
            collect(step * way)
    collect(0)
    for step in (3, 4,):
        for way in (1, -1):
            relay(step + 4, way).wait_recv()
            at = share(step + 4, way)
            k = step - 3 + (0 if way > 0 else len(FAR))
            near_sum = owner_out[step * way % Z, at].astype(F32) + relay_in[k, at].astype(F32)
            owner_out[step * way % Z, at] = near_sum.astype(BF16)
            copy = direct(step, way)
            copy.start()
            arrivals.append(copy)
    for copy in sum(a_copies, []) + sum(b_copies, []) + second:
        copy.wait_send()
    for copy in arrivals:
        copy.wait_recv()
    owner_copies += arrivals
    for e in range(4):
        near = {0: (4, 12), 1: (1, 5, 13), 2: (2, 6, 10, 14), 3: (3, 11, 15)}[e]
        value = owner_out[0].astype(F32) if e == 0 else None
        for k in near:
            more = owner_in[k].astype(F32)
            value = more if value is None else value + more
        row = pl.multiple_of(lax.rem(z - e + Z, 4) * 8, 8)
        for q in range(12):
            final_out[q // CAP, q % CAP, pl.ds(row, 8)] = value[8 * q : 8 * q + 8]
    block_rows = pl.ds(pl.multiple_of(x * 32, 32), 32)
    final = [
        send(final_out.at[lax.rem(x + s, X)], out.at[:, block_rows], fs.at[s - 1], fr.at[s - 1],
             x_peer(x, z, t, s))
        for s in (1, 3, 2)
    ]
    for copy in final:
        copy.start()
    out[:, block_rows] = final_out[x]
    for copy in final:
        copy.wait_recv()
    done = owner_copies + final
    for copy in done:
        copy.wait_send()


def local(tokens, hidden_grad, masters, block_row, block_col, owners):
    size_a, size_b = FIRST * 16, (KP - FIRST) * 16
    columns = hidden_grad.shape[1] // B
    result = pl.pallas_call(
        fused,
        name="fused",
        out_shape=pltpu.VMEM((CAP, B, B), F32),
        in_specs=[ANY, ANY, ANY, ANY, ANY, ANY],
        out_specs=VMEM,
        scratch_shapes=[
            pltpu.VMEM(block_row.shape, jnp.int32),
            pltpu.VMEM(block_col.shape, jnp.int32),
            pltpu.VMEM(owners.shape, jnp.int32),
            pltpu.VMEM((B, B), BF16),
            pltpu.VMEM((Y * CORES * 8, B, B), BF16),
            pltpu.VMEM((Z, 2, LOW, 2 * B), BF16),
            pltpu.VMEM((X, Z, B - LOW, B), BF16),
            pltpu.VMEM((B, B), F32),
            pltpu.VMEM(tokens.shape, BF16),
            pltpu.VMEM(hidden_grad.shape, BF16),
            pltpu.VMEM((columns, B, B), BF16),
            pltpu.VMEM((8, 2 * B), jnp.int32),
            pltpu.SMEM((8, 2 * B), jnp.int32),
            pltpu.VMEM((KP, B, 2 * B), F32),
            pltpu.VMEM((KP + 1, B, 2 * B), F32),
            pltpu.VMEM((16, size_a, B), BF16),
            pltpu.VMEM((16, size_b, B), BF16),
            pltpu.VMEM((4, 3, size_a, B), BF16),
            pltpu.VMEM((4, 3, size_b, B), BF16),
            pltpu.VMEM((3, size_a, B), BF16),
            pltpu.VMEM((3, size_b, B), BF16),
            pltpu.VMEM((3, size_a, B), BF16),
            pltpu.VMEM((3, size_b, B), BF16),
            pltpu.VMEM((2 * KP + 1, 8, B), F32),
            pltpu.VMEM((Z, 96, B), BF16),
            pltpu.VMEM((Z, 96, B), BF16),
            pltpu.VMEM((4, 96, B), BF16),
            pltpu.VMEM((X, CAP, 32, B), F32),
            DMA((7,)),
            DMA((3,)), DMA((3,)), DMA((Z,)), DMA((Z,)), DMA((Z,)), DMA((Z,)), DMA((Z, 3)), DMA((Z, 3)),
            DMA((3,)), DMA((3,)), DMA((4,)), DMA((4,)),
            DMA((4, 3)), DMA((4, 3)), DMA((4, 3)), DMA((4, 3)), DMA((4,)), DMA((4,)), DMA((3,)), DMA((3,)),
            DMA((Z,)), DMA((Z,)), DMA((4,)), DMA((4,)), DMA((3,)), DMA((3,)),
        ],
        compiler_params=pltpu.CompilerParams(
            collective_id=0, has_side_effects=True, vmem_limit_bytes=56 << 20
        ),
    )(tokens, hidden_grad, masters.reshape(B, B), block_row, block_col, owners)
    return result[None]


def solution(mesh):
    return jax.shard_map(
        local,
        mesh=mesh,
        in_specs=(
            P("dp", "tensor"),
            P("dp", "tensor"),
            P("tensor", "dp", None, None),
            P("tensor", None),
            P("tensor", None),
            P("tensor", None),
        ),
        out_specs=P("tensor", "dp", None, None),
        check_vma=False,
    )
```
